32 devices in a mesh: gx: 4 (over z), gz: 8 (over y, x, core).
Axes of the slice: x: 2, y: 2, z: 4, core: 2. Of those that a mesh axis runs over, the one named last changes fastest.
Arguments:
- fields: float32 [2, 16, 512, 512], P(None, 'gz', 'gx'), may hold values from -6 to 6
- grain_ids: int32 [16, 512, 512], P('gz', 'gx'), may hold values from 0 to 31, as said below
- grain_rates: float32 [32, 2], replicated, may hold values from 0.5 to 2.5
- die_mask: int32 [512, 512], P('gx'), may hold values from 0 to 1, as said below
Outputs:
- updated: float32 [2, 16, 512, 512], P(None, 'gz', 'gx')
The draws below stay inside these ranges and needn't reach their ends.
Inputs may be any that keep to these rules, and one draw needn't show every extreme that they name: `grain_ids`: grain ids are constant on aligned blocks of 2 cells along z by 8 by 8 cells along x and y. `die_mask`: the mask is constant on aligned blocks of 16 by 16 cells.
All inputs are finite; a program needn't handle non-finite values.
Results may differ from the reference program's by a relative error of at most 0.0003.
Values sent between devices are 32-bit elements; how exact they have to be, the bound alone decides.
No kernel may reach another device: no remote copies, remote signals or barrier semaphores. Data moves between devices by JAX's collectives and lax.ppermute only.
A program may use at most 128 MiB of HBM per device.

```python
import jax
import jax.numpy as jnp
from jax import lax

NX = 512
NY = 512
GRAINS = 32
NZ = 16


def draw_fields(key, part):
    full_shape = (2, NZ, NX, NY)
    return jnp.clip(jax.random.normal(key, full_shape, jnp.float32), -4.0, 4.0)


def draw_grain_ids(key, part):
    coarse = jax.random.randint(key, (NZ // 2, NX // 8, NY // 8), 0, GRAINS, dtype=jnp.int32)
    return jnp.repeat(jnp.repeat(jnp.repeat(coarse, 2, axis=0), 8, axis=1), 8, axis=2)


def draw_die_mask(key, part):
    coarse = jax.random.randint(key, (NX // 16, NY // 16), 0, 2, dtype=jnp.int32)
    return jnp.repeat(jnp.repeat(coarse, 16, axis=0), 16, axis=1)


def setup_inputs(seed: int = 0) -> dict:
    arg_keys = jax.random.split(jax.random.key(seed), 5)
    fields = draw_fields(jax.random.fold_in(arg_keys[4], 71), 0)
    grain_ids = draw_grain_ids(jax.random.fold_in(arg_keys[4], 71), 0)
    grain_rates = jnp.clip(jax.random.uniform(arg_keys[2], (GRAINS, 2), jnp.float32, 0.5, 2.5), 0.5, 2.5)
    die_mask = draw_die_mask(jax.random.fold_in(arg_keys[4], 71), 0)
    return dict(fields=fields, grain_ids=grain_ids, grain_rates=grain_rates, die_mask=die_mask)


heat_loss = 4.0
spread_solute = 2.0
spread_heat = 100.0


def line_solve(wave_real, wave_imag, mode_values, spread):
    layers = wave_real.shape[0]
    base_diag = 1.0 + spread * mode_values + 2.0 * spread
    row_ids = jnp.arange(layers, dtype=jnp.int32)

    def forward(carried, inputs):
        pivot_prev, prev_real, prev_imag = carried
        row_id, rhs_real, rhs_imag = inputs
        at_ends = jnp.logical_or(row_id == 0, row_id == layers - 1)
        diagonal = base_diag - jnp.where(at_ends, spread, 0.0)
        denominator = diagonal + spread * pivot_prev
        upper_coef = jnp.where(row_id == layers - 1, 0.0, -spread)
        pivot_now = upper_coef / denominator
        value_real = (rhs_real + spread * prev_real) / denominator
        value_imag = (rhs_imag + spread * prev_imag) / denominator
        return (pivot_now, value_real, value_imag), (pivot_now, value_real, value_imag)

    blank_plane = jnp.zeros(mode_values.shape, jnp.float32)
    unused, (pivots, values_real, values_imag) = lax.scan(forward, (blank_plane, blank_plane, blank_plane), (row_ids, wave_real, wave_imag))

    def backward(carried, inputs):
        above_real, above_imag = carried
        pivot_now, value_real, value_imag = inputs
        now_real = value_real - pivot_now * above_real
        now_imag = value_imag - pivot_now * above_imag
        return (now_real, now_imag), (now_real, now_imag)

    unused, (out_real, out_imag) = lax.scan(backward, (blank_plane, blank_plane), (pivots, values_real, values_imag), reverse=True)
    return out_real, out_imag


def reference(fields, grain_ids, grain_rates, die_mask):
    solute = fields[0]
    heat_now = fields[1]
    rate_solute = grain_rates[:, 0][grain_ids]
    rate_heat = grain_rates[:, 1][grain_ids]
    rhs_solute = solute + rate_solute * jnp.tanh(heat_now - solute)
    rhs_heat = heat_now + rate_heat * solute * solute / (1.0 + solute * solute)
    contact = die_mask.astype(jnp.float32)
    rhs_heat = rhs_heat.at[0].add(-(heat_loss * contact * (heat_now[0] + 1.0)))
    wave_x = jnp.arange(NX, dtype=jnp.int32).astype(jnp.float32)
    wave_y = jnp.arange(NY, dtype=jnp.int32).astype(jnp.float32)
    mode_values = 4.0 * jnp.sin(jnp.pi * wave_x / NX)[:, None] ** 2 + 4.0 * jnp.sin(jnp.pi * wave_y / NY)[None, :] ** 2
    results = []
    for rhs_field, spread in ((rhs_solute, spread_solute), (rhs_heat, spread_heat)):
        spectrum = jnp.fft.fft2(rhs_field, axes=(1, 2))
        solved_real, solved_imag = line_solve(jnp.real(spectrum).astype(jnp.float32), jnp.imag(spectrum).astype(jnp.float32), mode_values, spread)
        inverse = jnp.fft.ifft2(lax.complex(solved_real, solved_imag), axes=(1, 2))
        results.append(jnp.real(inverse).astype(jnp.float32))
    return jnp.stack(results)
```

```python
import math

import numpy as np
import jax
import jax.numpy as jnp
from jax import lax
from jax.experimental import pallas as pl
from jax.experimental.pallas import tpu as pltpu
from jax.sharding import PartitionSpec as P

heat_loss = 4.0
spread_solute = 2.0
spread_heat = 100.0
SUB = 8
LANES = 128
VMEM_LIMIT = 48 * 1024 * 1024


def split_tables(n):
    half = n // 2
    y = np.arange(half)
    cols, freq = [], []
    for j in range(half // 2 + 1):
        k = 2 * j
        scale = math.sqrt((1.0 if k in (0, half) else 2.0) / n)
        cols.append(scale * np.cos(2 * np.pi * k * y / n))
        freq.append(k)
        if 0 < j < half // 2:
            cols.append(scale * np.sin(2 * np.pi * k * y / n))
            freq.append(k)
    even = np.stack(cols, 1)
    cols, odd_freq = [], []
    for j in range(half // 2):
        k = 2 * j + 1
        scale = math.sqrt(2.0 / n)
        cols.append(scale * np.cos(2 * np.pi * k * y / n))
        cols.append(scale * np.sin(2 * np.pi * k * y / n))
        odd_freq += [k, k]
    odd = np.stack(cols, 1)
    eig = 4.0 * np.sin(np.pi * np.array(freq + odd_freq) / n) ** 2
    return even, odd, eig.astype(np.float32)


def hi_lo(a):
    hi = jnp.asarray(a, jnp.float32).astype(jnp.bfloat16)
    lo = (jnp.asarray(a, jnp.float32) - hi.astype(jnp.float32)).astype(jnp.bfloat16)
    return hi, lo


def table_pair(a):
    bf16 = jnp.bfloat16
    hi = a.astype(np.float32).astype(bf16)
    lo = (a - hi.astype(np.float64)).astype(np.float32).astype(bf16)
    return hi, lo


def dot3(x, q_hi, q_lo, dims):
    hi, lo = hi_lo(x)
    dn = (dims, ((), ()))
    f32 = jnp.float32
    return (
        lax.dot_general(hi, q_hi, dn, preferred_element_type=f32)
        + lax.dot_general(hi, q_lo, dn, preferred_element_type=f32)
        + lax.dot_general(lo, q_hi, dn, preferred_element_type=f32)
    )


def cosine_forward(v):
    n = len(v)
    if n == 1:
        return [v[0]]
    h = n // 2
    sums = [v[z] + v[n - 1 - z] for z in range(h)]
    diffs = [v[z] - v[n - 1 - z] for z in range(h)]
    even = cosine_forward(sums)
    out = [None] * n
    for j in range(h):
        out[2 * j] = even[j]
        k = 2 * j + 1
        acc = None
        for z in range(h):
            term = diffs[z] * float(math.cos(math.pi * k * (z + 0.5) / n))
            acc = term if acc is None else acc + term
        out[k] = acc
    return out


def cosine_backward(c):
    n = len(c)
    if n == 1:
        return [c[0]]
    h = n // 2
    even = cosine_backward([c[2 * j] for j in range(h)])
    out = [None] * n
    for z in range(h):
        acc = None
        for j in range(h):
            k = 2 * j + 1
            term = c[k] * float(math.cos(math.pi * k * (z + 0.5) / n))
            acc = term if acc is None else acc + term
        out[z] = even[z] + acc
        out[n - 1 - z] = even[z] - acc
    return out


def line_factors(eig_rows, spread, layer_eig):
    rest = 1.0 + spread * (eig_rows + layer_eig)
    root = jnp.sqrt(rest * (rest + 4.0 * spread))
    decay = 2.0 * spread / (rest + 2.0 * spread + root)
    return decay, root


def power(base, exponent):
    out = None
    square = base
    while exponent:
        if exponent & 1:
            out = square if out is None else out * square
        exponent >>= 1
        if exponent:
            square = square * square
    return out


def sublane_powers(step_decay, row, reverse):
    out = jnp.ones_like(step_decay)
    factor = step_decay
    place = (SUB - 1 - row) if reverse else row
    for bit in range(3):
        out = jnp.where((place >> bit) & 1 == 1, out * factor, out)
        factor = factor * factor
    return out


def on_device_fn(fields, grain_ids, grain_rates, die_mask):
    depth = fields.shape[1]
    local_x = fields.shape[2]
    span_y = fields.shape[3]
    half = span_y // 2
    devices_x = lax.axis_size("gx")
    devices_z = lax.axis_size("gz")
    layers = depth * devices_z
    chunks = devices_z // 2
    lanes = span_y // chunks
    steps = local_x // SUB
    tiles = span_y // LANES
    grain_count = grain_rates.shape[0]
    even, odd, eig = split_tables(span_y)
    even_hi, even_lo = table_pair(even)
    odd_hi, odd_lo = table_pair(odd)
    tables = [jnp.asarray(t) for t in (even_hi, even_lo, odd_hi, odd_lo)]
    eig_table = jnp.asarray(eig.reshape(chunks, lanes))
    f32 = jnp.float32
    params = pltpu.CompilerParams(vmem_limit_bytes=VMEM_LIMIT)
    piece = (depth, steps, SUB, lanes)
    grain_run = min(steps, 8)
    mask_run = min(steps, 16)

    def source_kernel(rates, *rest):
        f_refs, id_refs, mask_refs = rest[:tiles], rest[tiles : 2 * tiles], rest[2 * tiles : 3 * tiles]
        eh, el, oh, ol = rest[3 * tiles : 3 * tiles + 4]
        outs = rest[3 * tiles + 4 : 3 * tiles + 4 + devices_z]
        sums, diffs, modes = rest[3 * tiles + 4 + devices_z :]
        g = lax.axis_index("gz")
        layer = pl.program_id(0)
        first = jnp.where(g * depth + layer == 0, heat_loss, 0.0)
        for tile in range(tiles // 2):
            pair = (tile, tile + tiles // 2)
            rates_c, rates_h, sinks = [None] * 2, [None] * 2, [None] * 2
            for xi in range(steps):
                at = pl.ds(xi, SUB, stride=steps)
                rhs = [[None] * 2, [None] * 2]
                for side in range(2):
                    if xi % grain_run == 0:
                        ids = id_refs[pair[side]][0, at, :]
                        rate_c = jnp.zeros(ids.shape, f32)
                        rate_h = jnp.zeros(ids.shape, f32)
                        for grain in range(grain_count):
                            hit = ids == grain
                            rate_c = jnp.where(hit, rates[grain, 0], rate_c)
                            rate_h = jnp.where(hit, rates[grain, 1], rate_h)
                        rates_c[side], rates_h[side] = rate_c, rate_h
                    if xi % mask_run == 0:
                        sinks[side] = mask_refs[pair[side]][at, :].astype(f32) * first
                    c = f_refs[pair[side]][0, 0, at, :]
                    h = f_refs[pair[side]][1, 0, at, :]
                    square = c * c
                    rhs[0][side] = c + rates_c[side] * jnp.tanh(h - c)
                    rhs[1][side] = (
                        h + rates_h[side] * square / (1.0 + square) - sinks[side] * (h + 1.0)
                    )
                for f in range(2):
                    rows = pl.ds((f * steps + xi) * SUB, SUB)
                    cols = pl.ds(tile * LANES, LANES)
                    sums[rows, cols] = rhs[f][0] + rhs[f][1]
                    diffs[rows, cols] = rhs[f][0] - rhs[f][1]
        dims = ((1,), (0,))
        for f in range(2):
            rows = pl.ds(f * local_x, local_x)
            both = (
                dot3(sums[rows, :], eh[...], el[...], dims),
                dot3(diffs[rows, :], oh[...], ol[...], dims),
            )
            for chunk in range(chunks):
                part = both[chunk * lanes // half]
                at = chunk * lanes % half
                modes[2 * chunk + f] = part[:, at : at + lanes].reshape(steps, SUB, lanes)
        for k in range(devices_z):
            outs[k][0] = modes[g ^ k]

    whole = lambda shape: pl.BlockSpec(shape, lambda i: (0,) * len(shape))
    id_step = 2 if depth % 2 == 0 else 1
    pieces = pl.pallas_call(
        source_kernel,
        grid=(depth,),
        in_specs=[
            pl.BlockSpec(memory_space=pltpu.SMEM),
        ]
        + [
            pl.BlockSpec((2, 1, local_x, LANES), lambda i, t=t: (0, i, 0, t))
            for t in range(tiles)
        ]
        + [
            pl.BlockSpec((1, local_x, LANES), lambda i, t=t: (i // id_step * id_step, 0, t))
            for t in range(tiles)
        ]
        + [pl.BlockSpec((local_x, LANES), lambda i, t=t: (0, t)) for t in range(tiles)]
        + [whole((half, half))] * 4,
        out_specs=[pl.BlockSpec((1, steps, SUB, lanes), lambda i: (i, 0, 0, 0))] * devices_z,
        out_shape=[jax.ShapeDtypeStruct(piece, f32)] * devices_z,
        scratch_shapes=[
            pltpu.VMEM((2 * local_x, half), f32),
            pltpu.VMEM((2 * local_x, half), f32),
            pltpu.VMEM((devices_z, steps, SUB, lanes), f32),
        ],
        compiler_params=params,
        name="sources",
    )(grain_rates, *([fields] * tiles + [grain_ids] * tiles + [die_mask] * tiles), *tables)

    def exchange(arrays, axis):
        count = lax.axis_size(axis)
        out = [arrays[0]]
        for k in range(1, count):
            out.append(lax.ppermute(arrays[k], axis, [(i, i ^ k) for i in range(count)]))
        return out

    gathered = exchange(pieces, "gz")

    def line_setup(eig_ref):
        g = lax.axis_index("gz")
        spread = jnp.where(g % 2 == 0, spread_solute, spread_heat).astype(f32)
        eig_rows = jnp.broadcast_to(eig_ref[pl.ds(g // 2, 1), :], (SUB, lanes))
        return g, spread, eig_rows

    layer_eig = [4.0 * math.sin(math.pi * k / (2 * layers)) ** 2 for k in range(layers)]

    def gather_kernel(eig_ref, *rest):
        ins = rest[: devices_z]
        hat_ref, from_left, from_right, ends, field, sems = rest[devices_z :]
        g, spread, eig_rows = line_setup(eig_ref)
        copies = []
        for k in range(devices_z):
            copies.append(
                pltpu.make_async_copy(ins[k], field.at[pl.ds((g ^ k) * depth, depth)], sems.at[k])
            )
            copies[-1].start()
        for copy in copies:
            copy.wait()

        def transform(xi, carry):
            hat = cosine_forward([field[z, xi] for z in range(layers)])
            for k in range(layers):
                hat_ref[k, xi] = hat[k]
            return carry

        lax.fori_loop(0, steps, transform, 0)
        row = lax.broadcasted_iota(jnp.int32, (SUB, lanes), 0)
        for k in range(layers):
            decay, _ = line_factors(eig_rows, spread, layer_eig[k])
            left = hat_ref[k, 0]
            right = hat_ref[k, steps - 1]
            for xi in range(1, steps):
                left = hat_ref[k, xi] + decay * left
                right = hat_ref[k, steps - 1 - xi] + decay * right
            step_decay = power(decay, steps)
            up = sublane_powers(step_decay, row, False)
            down = sublane_powers(step_decay, row, True)
            ends[0, pl.ds(k, 1), :] = jnp.sum(left * down, axis=0, keepdims=True)
            ends[1, pl.ds(k, 1), :] = jnp.sum(right * up, axis=0, keepdims=True)
            left = jnp.where(row >= 1, pltpu.roll(left, 1, 0), 0.0)
            right = jnp.where(row < SUB - 1, pltpu.roll(right, SUB - 1, 0), 0.0)
            factor = step_decay
            for shift in (1, 2, 4):
                left = left + factor * jnp.where(row >= shift, pltpu.roll(left, shift, 0), 0.0)
                right = right + factor * jnp.where(
                    row < SUB - shift, pltpu.roll(right, SUB - shift, 0), 0.0
                )
                factor = factor * factor
            from_left[k] = left
            from_right[k] = right

    vmem = pl.BlockSpec(memory_space=pltpu.VMEM)
    anywhere = pl.BlockSpec(memory_space=pl.ANY)
    hat, from_left, from_right, ends = pl.pallas_call(
        gather_kernel,
        in_specs=[vmem] + [anywhere] * devices_z,
        out_specs=[vmem] * 4,
        out_shape=[
            jax.ShapeDtypeStruct((layers, steps, SUB, lanes), f32),
            jax.ShapeDtypeStruct((layers, SUB, lanes), f32),
            jax.ShapeDtypeStruct((layers, SUB, lanes), f32),
            jax.ShapeDtypeStruct((2, layers, lanes), f32),
        ],
        scratch_shapes=[
            pltpu.VMEM((layers, steps, SUB, lanes), f32),
            pltpu.SemaphoreType.DMA((devices_z,)),
        ],
        compiler_params=params,
        name="gather",
    )(eig_table, *gathered)

    all_ends = exchange([ends] * devices_x, "gx")

    def solve_kernel(eig_ref, hat_ref, left_ref, right_ref, *rest):
        end_refs = rest[: devices_x]
        outs = rest[devices_x : devices_x + devices_z]
        near, work, entry, end_sems, sems = rest[devices_x + devices_z :]
        g, spread, eig_rows = line_setup(eig_ref)
        place = lax.axis_index("gx")
        copies = []
        for k in range(devices_x):
            copies.append(pltpu.make_async_copy(end_refs[k], near.at[place ^ k], end_sems.at[k]))
            copies[-1].start()
        for copy in copies:
            copy.wait()
        row = lax.broadcasted_iota(jnp.int32, (SUB, lanes), 0)
        eig_one = eig_ref[pl.ds(g // 2, 1), :]
        kz = lax.broadcasted_iota(jnp.int32, (layers, lanes), 0).astype(f32)
        eig_z = 4.0 * jnp.sin(kz * (math.pi / (2 * layers))) ** 2
        decay_all, _ = line_factors(eig_one, spread, eig_z)
        block_decay = power(decay_all, local_x)
        total_left = near[(place + devices_x - 1) % devices_x, 0]
        total_right = near[(place + 1) % devices_x, 1]
        weight = block_decay
        for m in range(2, devices_x + 1):
            total_left = total_left + weight * near[(place + devices_x - m) % devices_x, 0]
            total_right = total_right + weight * near[(place + m) % devices_x, 1]
            weight = weight * block_decay
        entry[0] = total_left / (1.0 - weight)
        entry[1] = total_right / (1.0 - weight)
        for k in range(layers):
            decay, root = line_factors(eig_rows, spread, layer_eig[k])
            gain = ((1.0 if k == 0 else 2.0) / layers) / root
            step_decay = power(decay, steps)
            up = sublane_powers(step_decay, row, False)
            down = sublane_powers(step_decay, row, True)
            left = left_ref[k] + up * entry[0, pl.ds(k, 1), :]
            right = right_ref[k] + down * entry[1, pl.ds(k, 1), :]
            for xi in range(steps):
                left = hat_ref[k, xi] + decay * left
                work[k, xi] = left
            for xi in reversed(range(steps)):
                carried = decay * right
                work[k, xi] = gain * (work[k, xi] + carried)
                right = hat_ref[k, xi] + carried

        def back(xi, carry):
            values = cosine_backward([work[k, xi] for k in range(layers)])
            for z in range(layers):
                work[z, xi] = values[z]
            return carry

        lax.fori_loop(0, steps, back, 0)
        copies = []
        for k in range(devices_z):
            copies.append(
                pltpu.make_async_copy(work.at[pl.ds((g ^ k) * depth, depth)], outs[k], sems.at[k])
            )
            copies[-1].start()
        for copy in copies:
            copy.wait()

    solved = pl.pallas_call(
        solve_kernel,
        in_specs=[vmem] * 4 + [anywhere] * devices_x,
        out_specs=[anywhere] * devices_z,
        out_shape=[jax.ShapeDtypeStruct(piece, f32)] * devices_z,
        scratch_shapes=[
            pltpu.VMEM((devices_x, 2, layers, lanes), f32),
            pltpu.VMEM((layers, steps, SUB, lanes), f32),
            pltpu.VMEM((2, layers, lanes), f32),
            pltpu.SemaphoreType.DMA((devices_x,)),
            pltpu.SemaphoreType.DMA((devices_z,)),
        ],
        compiler_params=params,
        name="solve",
    )(eig_table, hat, from_left, from_right, *all_ends)

    returned = exchange(solved, "gz")

    def final_kernel(eh, el, oh, ol, *rest):
        ins = rest[: devices_z]
        out_ref, modes, buf, sems, out_sems = rest[devices_z :]
        g = lax.axis_index("gz")
        step = pl.program_id(0)

        @pl.when(step == 0)
        def _():
            copies = []
            for k in range(devices_z):
                copies.append(pltpu.make_async_copy(ins[k], modes.at[g ^ k], sems.at[k]))
                copies[-1].start()
            for copy in copies:
                copy.wait()

        f = step // depth
        layer = step % depth
        parts = [
            modes[2 * chunk + f, layer].reshape(local_x, lanes) for chunk in range(chunks)
        ]
        dims = ((1,), (1,))
        low = dot3(jnp.concatenate(parts[: chunks // 2], axis=1), eh[...], el[...], dims)
        high = dot3(jnp.concatenate(parts[chunks // 2 :], axis=1), oh[...], ol[...], dims)
        total = low + high
        other = low - high
        slot = step % 2

        def out_copies(step, slot):
            where = out_ref.at[step // depth, step % depth]
            return [
                pltpu.make_async_copy(
                    buf.at[slot, t], where.at[:, pl.ds(t * LANES, LANES)], out_sems.at[slot, t]
                )
                for t in range(tiles)
            ]

        @pl.when(step >= 2)
        def _():
            for copy in out_copies(step - 2, slot):
                copy.wait()

        for t in range(tiles):
            value = total if t < tiles // 2 else other
            at = t % (tiles // 2) * LANES
            for xi in range(steps):
                buf[slot, t, pl.ds(xi, SUB, stride=steps), :] = value[
                    xi * SUB : xi * SUB + SUB, at : at + LANES
                ]
        for copy in out_copies(step, slot):
            copy.start()

        @pl.when(step == 2 * depth - 1)
        def _():
            for back in (1, 0):
                for copy in out_copies(step - back, (step - back) % 2):
                    copy.wait()

    return pl.pallas_call(
        final_kernel,
        grid=(2 * depth,),
        in_specs=[whole((half, half))] * 4 + [anywhere] * devices_z,
        out_specs=anywhere,
        out_shape=jax.ShapeDtypeStruct((2, depth, local_x, span_y), f32),
        scratch_shapes=[
            pltpu.VMEM((devices_z, depth, steps, SUB, lanes), f32),
            pltpu.VMEM((2, tiles, local_x, LANES), f32),
            pltpu.SemaphoreType.DMA((devices_z,)),
            pltpu.SemaphoreType.DMA((2, tiles)),
        ],
        compiler_params=params,
        name="finish",
    )(*tables, *returned)


def solution(mesh):
    placed = (P(None, "gz", "gx", None), P("gz", "gx", None), P(), P("gx", None))
    return jax.shard_map(
        on_device_fn, mesh=mesh, in_specs=placed, out_specs=P(None, "gz", "gx", None), check_vma=False
    )
```

```python
import math

import numpy as np
import jax
import jax.numpy as jnp
from jax import lax
from jax.experimental import pallas as pl
from jax.experimental.pallas import tpu as pltpu
from jax.sharding import PartitionSpec as P

heat_loss = 4.0
spread_solute = 2.0
spread_heat = 100.0
SUB = 8
LANES = 128
VMEM_LIMIT = 48 * 1024 * 1024


def split_tables(n):
    half = n // 2
    y = np.arange(half)
    cols, freq = [], []
    for j in range(half // 2 + 1):
        k = 2 * j
        scale = math.sqrt((1.0 if k in (0, half) else 2.0) / n)
        cols.append(scale * np.cos(2 * np.pi * k * y / n))
        freq.append(k)
        if 0 < j < half // 2:
            cols.append(scale * np.sin(2 * np.pi * k * y / n))
            freq.append(k)
    even = np.stack(cols, 1)
    cols, odd_freq = [], []
    for j in range(half // 2):
        k = 2 * j + 1
        scale = math.sqrt(2.0 / n)
        cols.append(scale * np.cos(2 * np.pi * k * y / n))
        cols.append(scale * np.sin(2 * np.pi * k * y / n))
        odd_freq += [k, k]
    odd = np.stack(cols, 1)
    eig = 4.0 * np.sin(np.pi * np.array(freq + odd_freq) / n) ** 2
    return even, odd, eig.astype(np.float32)


def hi_lo(a):
    hi = jnp.asarray(a, jnp.float32).astype(jnp.bfloat16)
    lo = (jnp.asarray(a, jnp.float32) - hi.astype(jnp.float32)).astype(jnp.bfloat16)
    return hi, lo


def table_pair(a):
    bf16 = jnp.bfloat16
    hi = a.astype(np.float32).astype(bf16)
    lo = (a - hi.astype(np.float64)).astype(np.float32).astype(bf16)
    return hi, lo


def dot3(x, q_hi, q_lo, dims):
    hi, lo = hi_lo(x)
    dn = (dims, ((), ()))
    f32 = jnp.float32
    return (
        lax.dot_general(hi, q_hi, dn, preferred_element_type=f32)
        + lax.dot_general(hi, q_lo, dn, preferred_element_type=f32)
        + lax.dot_general(lo, q_hi, dn, preferred_element_type=f32)
    )


def cosine_forward(v):
    n = len(v)
    if n == 1:
        return [v[0]]
    h = n // 2
    sums = [v[z] + v[n - 1 - z] for z in range(h)]
    diffs = [v[z] - v[n - 1 - z] for z in range(h)]
    even = cosine_forward(sums)
    out = [None] * n
    for j in range(h):
        out[2 * j] = even[j]
        k = 2 * j + 1
        acc = None
        for z in range(h):
            term = diffs[z] * float(math.cos(math.pi * k * (z + 0.5) / n))
            acc = term if acc is None else acc + term
        out[k] = acc
    return out


def cosine_backward(c):
    n = len(c)
    if n == 1:
        return [c[0]]
    h = n // 2
    even = cosine_backward([c[2 * j] for j in range(h)])
    out = [None] * n
    for z in range(h):
        acc = None
        for j in range(h):
            k = 2 * j + 1
            term = c[k] * float(math.cos(math.pi * k * (z + 0.5) / n))
            acc = term if acc is None else acc + term
        out[z] = even[z] + acc
        out[n - 1 - z] = even[z] - acc
    return out


def line_factors(eig_rows, spread, layer_eig):
    rest = 1.0 + spread * (eig_rows + layer_eig)
    root = jnp.sqrt(rest * (rest + 4.0 * spread))
    decay = 2.0 * spread / (rest + 2.0 * spread + root)
    return decay, root


def power(base, exponent):
    out = None
    square = base
    while exponent:
        if exponent & 1:
            out = square if out is None else out * square
        exponent >>= 1
        if exponent:
            square = square * square
    return out


def sublane_powers(step_decay, row, reverse):
    out = jnp.ones_like(step_decay)
    factor = step_decay
    place = (SUB - 1 - row) if reverse else row
    for bit in range(3):
        out = jnp.where((place >> bit) & 1 == 1, out * factor, out)
        factor = factor * factor
    return out


def on_device_fn(fields, grain_ids, grain_rates, die_mask):
    depth = fields.shape[1]
    local_x = fields.shape[2]
    span_y = fields.shape[3]
    half = span_y // 2
    devices_x = lax.axis_size("gx")
    devices_z = lax.axis_size("gz")
    layers = depth * devices_z
    chunks = devices_z // 2
    lanes = span_y // chunks
    steps = local_x // SUB
    tiles = span_y // LANES
    grain_count = grain_rates.shape[0]
    even, odd, eig = split_tables(span_y)
    even_hi, even_lo = table_pair(even)
    odd_hi, odd_lo = table_pair(odd)
    tables = [jnp.asarray(t) for t in (even_hi, even_lo, odd_hi, odd_lo)]
    back_tables = [jnp.asarray(np.ascontiguousarray(t.T)) for t in (even_hi, even_lo, odd_hi, odd_lo)]
    eig_table = jnp.asarray(eig.reshape(chunks, lanes))
    f32 = jnp.float32
    params = pltpu.CompilerParams(vmem_limit_bytes=VMEM_LIMIT)
    piece = (depth, steps, SUB, lanes)
    grain_run = min(steps, 8)
    mask_run = min(steps, 16)

    vmem = pl.BlockSpec(memory_space=pltpu.VMEM)
    hbm = pl.BlockSpec(memory_space=pltpu.HBM)
    shared = 2 if depth % 2 == 0 else 1

    def source_kernel(rates_hbm, f_hbm, id_hbm, mask_hbm, eh_hbm, el_hbm, oh_hbm, ol_hbm, *rest):
        outs = rest[:devices_z]
        f_buf, id_buf, mask_buf, sums, diffs, modes, eh, el, oh, ol, rates = rest[devices_z:-3]
        f_sems, tile_sems, table_sems = rest[-3:]
        g = lax.axis_index("gz")
        field_copies = [
            pltpu.make_async_copy(
                f_hbm.at[:, layer, :, pl.ds(t * LANES, LANES)],
                f_buf.at[layer, t],
                f_sems.at[layer, t],
            )
            for layer in range(depth)
            for t in range(tiles)
        ]
        tile_copies = []
        for t in range(tiles):
            cols = pl.ds(t * LANES, LANES)
            for group in range(depth // shared):
                tile_copies.append(
                    pltpu.make_async_copy(
                        id_hbm.at[group * shared, :, cols],
                        id_buf.at[group, t],
                        tile_sems.at[0, group, t],
                    )
                )
            tile_copies.append(
                pltpu.make_async_copy(mask_hbm.at[:, cols], mask_buf.at[t], tile_sems.at[1, 0, t])
            )
        table_copies = [
            pltpu.make_async_copy(src, dst, table_sems.at[i])
            for i, (src, dst) in enumerate(
                ((eh_hbm, eh), (el_hbm, el), (oh_hbm, oh), (ol_hbm, ol))
            )
        ]
        tile_copies.append(pltpu.make_async_copy(rates_hbm, rates, table_sems.at[4]))
        for copy in tile_copies + field_copies + table_copies:
            copy.start()
        for copy in tile_copies:
            copy.wait()
        for layer in range(depth):
            first = jnp.where(g * depth + layer == 0, heat_loss, 0.0)
            for copy in field_copies[layer * tiles : (layer + 1) * tiles]:
                copy.wait()
            for tile in range(tiles // 2):
                pair = (tile, tile + tiles // 2)
                rates_c, rates_h, sinks = [None] * 2, [None] * 2, [None] * 2
                for xi in range(steps):
                    at = pl.ds(xi, SUB, stride=steps)
                    rhs = [[None] * 2, [None] * 2]
                    for side in range(2):
                        t = pair[side]
                        if xi % grain_run == 0:
                            ids = id_buf[layer // shared, t, at, :]
                            rate_c = jnp.zeros(ids.shape, f32)
                            rate_h = jnp.zeros(ids.shape, f32)
                            for grain in range(grain_count):
                                hit = ids == grain
                                rate_c = jnp.where(hit, rates[0, grain], rate_c)
                                rate_h = jnp.where(hit, rates[1, grain], rate_h)
                            rates_c[side], rates_h[side] = rate_c, rate_h
                        if xi % mask_run == 0:
                            sinks[side] = mask_buf[t, at, :].astype(f32) * first
                        c = f_buf[layer, t, 0, at, :]
                        h = f_buf[layer, t, 1, at, :]
                        square = c * c
                        rhs[0][side] = c + rates_c[side] * jnp.tanh(h - c)
                        rhs[1][side] = (
                            h + rates_h[side] * square / (1.0 + square) - sinks[side] * (h + 1.0)
                        )
                    for f in range(2):
                        rows = pl.ds((f * steps + xi) * SUB, SUB)
                        cols = pl.ds(tile * LANES, LANES)
                        sums[layer, rows, cols] = rhs[f][0] + rhs[f][1]
                        diffs[layer, rows, cols] = rhs[f][0] - rhs[f][1]
            if layer == 0:
                for copy in table_copies:
                    copy.wait()
            for parity, (src, hi, lo) in enumerate(((sums, eh, el), (diffs, oh, ol))):
                both = dot3(src[layer], hi[...], lo[...], ((1,), (0,)))
                for f in range(2):
                    for chunk in range(chunks // 2):
                        part = both[
                            f * local_x : (f + 1) * local_x, chunk * lanes : (chunk + 1) * lanes
                        ]
                        place = 2 * (chunk + parity * (chunks // 2)) + f
                        modes[place, layer] = part.reshape(steps, SUB, lanes)
        for k in range(devices_z):
            outs[k][...] = modes[g ^ k]

    square = (half, half)
    pieces = pl.pallas_call(
        source_kernel,
        in_specs=[hbm] * 8,
        out_specs=[vmem] * devices_z,
        out_shape=[jax.ShapeDtypeStruct(piece, f32)] * devices_z,
        scratch_shapes=[
            pltpu.VMEM((depth, tiles, 2, local_x, LANES), f32),
            pltpu.VMEM((depth // shared, tiles, local_x, LANES), jnp.int32),
            pltpu.VMEM((tiles, local_x, LANES), jnp.int32),
            pltpu.VMEM((depth, 2 * local_x, half), f32),
            pltpu.VMEM((depth, 2 * local_x, half), f32),
            pltpu.VMEM((devices_z,) + piece, f32),
        ]
        + [pltpu.VMEM(square, jnp.bfloat16)] * 4
        + [
            pltpu.SMEM((2, grain_count), f32),
            pltpu.SemaphoreType.DMA((depth, tiles)),
            pltpu.SemaphoreType.DMA((2, depth // shared, tiles)),
            pltpu.SemaphoreType.DMA((5,)),
        ],
        compiler_params=params,
        name="sources",
    )(
        *(
            pltpu.with_memory_space_constraint(a, pltpu.HBM)
            for a in (grain_rates.T, fields, grain_ids, die_mask, *tables)
        ),
    )

    def exchange(arrays, axis, order):
        count = lax.axis_size(axis)
        out = []
        for k in order:
            route = [(i, i ^ k) for i in range(count)]
            out.append(lax.ppermute(arrays[k], axis, route) if k else arrays[k])
        return out

    order_z = [0] + sorted(range(1, devices_z), key=lambda k: (k & 1, -k))
    order_x = list(range(devices_x))

    gathered = exchange(pieces, "gz", order_z)

    def line_setup(eig_ref):
        g = lax.axis_index("gz")
        spread = jnp.where(g % 2 == 0, spread_solute, spread_heat).astype(f32)
        eig_rows = jnp.broadcast_to(eig_ref[pl.ds(g // 2, 1), :], (SUB, lanes))
        return g, spread, eig_rows

    layer_eig = [4.0 * math.sin(math.pi * k / (2 * layers)) ** 2 for k in range(layers)]

    def gather_kernel(eig_ref, *rest):
        ins = rest[: devices_z]
        hat_ref, from_left, from_right, ends, field = rest[devices_z:]
        g, spread, eig_rows = line_setup(eig_ref)
        for i, k in enumerate(order_z):
            field[pl.ds((g ^ k) * depth, depth)] = ins[i][...]

        def transform(xi, carry):
            hat = cosine_forward([field[z, xi] for z in range(layers)])
            for k in range(layers):
                hat_ref[k, xi] = hat[k]
            return carry

        lax.fori_loop(0, steps, transform, 0)
        row = lax.broadcasted_iota(jnp.int32, (SUB, lanes), 0)
        for k in range(layers):
            decay, _ = line_factors(eig_rows, spread, layer_eig[k])
            left = hat_ref[k, 0]
            right = hat_ref[k, steps - 1]
            for xi in range(1, steps):
                left = hat_ref[k, xi] + decay * left
                right = hat_ref[k, steps - 1 - xi] + decay * right
            step_decay = power(decay, steps)
            up = sublane_powers(step_decay, row, False)
            down = sublane_powers(step_decay, row, True)
            ends[0, pl.ds(k, 1), :] = jnp.sum(left * down, axis=0, keepdims=True)
            ends[1, pl.ds(k, 1), :] = jnp.sum(right * up, axis=0, keepdims=True)
            left = jnp.where(row >= 1, pltpu.roll(left, 1, 0), 0.0)
            right = jnp.where(row < SUB - 1, pltpu.roll(right, SUB - 1, 0), 0.0)
            factor = step_decay
            for shift in (1, 2, 4):
                left = left + factor * jnp.where(row >= shift, pltpu.roll(left, shift, 0), 0.0)
                right = right + factor * jnp.where(
                    row < SUB - shift, pltpu.roll(right, SUB - shift, 0), 0.0
                )
                factor = factor * factor
            from_left[k] = left
            from_right[k] = right

    hat, from_left, from_right, ends = pl.pallas_call(
        gather_kernel,
        in_specs=[vmem] * (1 + devices_z),
        out_specs=[vmem] * 4,
        out_shape=[
            jax.ShapeDtypeStruct((layers, steps, SUB, lanes), f32),
            jax.ShapeDtypeStruct((layers, SUB, lanes), f32),
            jax.ShapeDtypeStruct((layers, SUB, lanes), f32),
            jax.ShapeDtypeStruct((2, layers, lanes), f32),
        ],
        scratch_shapes=[
            pltpu.VMEM((layers, steps, SUB, lanes), f32),
        ],
        compiler_params=params,
        name="gather",
    )(eig_table, *gathered)

    all_ends = exchange([ends] * devices_x, "gx", order_x)

    def solve_kernel(eig_ref, hat_ref, left_ref, right_ref, *rest):
        end_refs = rest[: devices_x]
        outs = rest[devices_x : devices_x + devices_z]
        near, work, entry = rest[devices_x + devices_z :]
        g, spread, eig_rows = line_setup(eig_ref)
        place = lax.axis_index("gx")
        for i, k in enumerate(order_x):
            near[place ^ k] = end_refs[i][...]
        row = lax.broadcasted_iota(jnp.int32, (SUB, lanes), 0)
        eig_one = eig_ref[pl.ds(g // 2, 1), :]
        kz = lax.broadcasted_iota(jnp.int32, (layers, lanes), 0).astype(f32)
        eig_z = 4.0 * jnp.sin(kz * (math.pi / (2 * layers))) ** 2
        decay_all, _ = line_factors(eig_one, spread, eig_z)
        block_decay = power(decay_all, local_x)
        total_left = near[(place + devices_x - 1) % devices_x, 0]
        total_right = near[(place + 1) % devices_x, 1]
        weight = block_decay
        for m in range(2, devices_x + 1):
            total_left = total_left + weight * near[(place + devices_x - m) % devices_x, 0]
            total_right = total_right + weight * near[(place + m) % devices_x, 1]
            weight = weight * block_decay
        entry[0] = total_left / (1.0 - weight)
        entry[1] = total_right / (1.0 - weight)
        for k in range(layers):
            decay, root = line_factors(eig_rows, spread, layer_eig[k])
            gain = ((1.0 if k == 0 else 2.0) / layers) / root
            step_decay = power(decay, steps)
            up = sublane_powers(step_decay, row, False)
            down = sublane_powers(step_decay, row, True)
            left = left_ref[k] + up * entry[0, pl.ds(k, 1), :]
            right = right_ref[k] + down * entry[1, pl.ds(k, 1), :]
            for xi in range(steps):
                left = hat_ref[k, xi] + decay * left
                work[k, xi] = left
            for xi in reversed(range(steps)):
                carried = decay * right
                work[k, xi] = gain * (work[k, xi] + carried)
                right = hat_ref[k, xi] + carried

        def back(xi, carry):
            values = cosine_backward([work[k, xi] for k in range(layers)])
            for z in range(layers):
                work[z, xi] = values[z]
            return carry

        lax.fori_loop(0, steps, back, 0)
        for k in range(devices_z):
            outs[k][...] = work[pl.ds((g ^ k) * depth, depth)]

    solved = pl.pallas_call(
        solve_kernel,
        in_specs=[vmem] * (4 + devices_x),
        out_specs=[vmem] * devices_z,
        out_shape=[jax.ShapeDtypeStruct(piece, f32)] * devices_z,
        scratch_shapes=[
            pltpu.VMEM((devices_x, 2, layers, lanes), f32),
            pltpu.VMEM((layers, steps, SUB, lanes), f32),
            pltpu.VMEM((2, layers, lanes), f32),
        ],
        compiler_params=params,
        name="solve",
    )(eig_table, hat, from_left, from_right, *all_ends)

    returned = exchange(solved, "gz", order_z)

    def final_kernel(eh, el, oh, ol, *rest):
        ins = rest[:devices_z]
        out_ref, modes, buf, out_sems = rest[devices_z:]
        g = lax.axis_index("gz")
        for i, k in enumerate(order_z):
            modes[g ^ k] = ins[i][...]
        copies = []
        dims = ((1,), (0,))
        for f in range(2):
            parts = [
                modes[2 * chunk + f].reshape(depth * local_x, lanes) for chunk in range(chunks)
            ]
            low = dot3(jnp.concatenate(parts[: chunks // 2], axis=1), eh[...], el[...], dims)
            high = dot3(jnp.concatenate(parts[chunks // 2 :], axis=1), oh[...], ol[...], dims)
            for side, value in enumerate((low + high, low - high)):
                for layer in range(depth):
                    for col in range(tiles // 2):
                        t = side * (tiles // 2) + col
                        for xi in range(steps):
                            at = (layer * steps + xi) * SUB
                            buf[f, layer, t, pl.ds(xi, SUB, stride=steps), :] = value[
                                at : at + SUB, col * LANES : (col + 1) * LANES
                            ]
                        copies.append(
                            pltpu.make_async_copy(
                                buf.at[f, layer, t],
                                out_ref.at[f, layer, :, pl.ds(t * LANES, LANES)],
                                out_sems.at[f, layer, t],
                            )
                        )
                        copies[-1].start()
        for copy in copies:
            copy.wait()

    return pl.pallas_call(
        final_kernel,
        in_specs=[vmem] * (4 + devices_z),
        out_specs=hbm,
        out_shape=jax.ShapeDtypeStruct((2, depth, local_x, span_y), f32),
        scratch_shapes=[
            pltpu.VMEM((devices_z,) + piece, f32),
            pltpu.VMEM((2, depth, tiles, local_x, LANES), f32),
            pltpu.SemaphoreType.DMA((2, depth, tiles)),
        ],
        compiler_params=params,
        name="finish",
    )(*back_tables, *returned)


def solution(mesh):
    placed = (P(None, "gz", "gx", None), P("gz", "gx", None), P(), P("gx", None))
    return jax.shard_map(
        on_device_fn, mesh=mesh, in_specs=placed, out_specs=P(None, "gz", "gx", None), check_vma=False
    )
```

```python
import functools
import math

import numpy as np
import jax
import jax.numpy as jnp
from jax import lax
from jax.experimental import pallas as pl
from jax.experimental.pallas import tpu as pltpu
from jax.sharding import PartitionSpec as P

heat_loss = 4.0
spread_solute = 2.0
spread_heat = 100.0
SUB = 8
LANES = 128
VMEM_LIMIT = 48 * 1024 * 1024


def split_tables(n):
    half = n // 2
    y = np.arange(half)
    cols, freq = [], []
    for j in range(half // 2 + 1):
        k = 2 * j
        scale = math.sqrt((1.0 if k in (0, half) else 2.0) / n)
        cols.append(scale * np.cos(2 * np.pi * k * y / n))
        freq.append(k)
        if 0 < j < half // 2:
            cols.append(scale * np.sin(2 * np.pi * k * y / n))
            freq.append(k)
    even = np.stack(cols, 1)
    cols, odd_freq = [], []
    for j in range(half // 2):
        k = 2 * j + 1
        scale = math.sqrt(2.0 / n)
        cols.append(scale * np.cos(2 * np.pi * k * y / n))
        cols.append(scale * np.sin(2 * np.pi * k * y / n))
        odd_freq += [k, k]
    odd = np.stack(cols, 1)
    eig = 4.0 * np.sin(np.pi * np.array(freq + odd_freq) / n) ** 2
    return even, odd, eig.astype(np.float32)


def hi_lo(a):
    hi = jnp.asarray(a, jnp.float32).astype(jnp.bfloat16)
    lo = (jnp.asarray(a, jnp.float32) - hi.astype(jnp.float32)).astype(jnp.bfloat16)
    return hi, lo


def table_pair(a):
    bf16 = jnp.bfloat16
    hi = a.astype(np.float32).astype(bf16)
    lo = (a - hi.astype(np.float64)).astype(np.float32).astype(bf16)
    return hi, lo


def dot3(x, q_hi, q_lo, dims):
    hi, lo = hi_lo(x)
    dn = (dims, ((), ()))
    f32 = jnp.float32
    return (
        lax.dot_general(hi, q_hi, dn, preferred_element_type=f32)
        + lax.dot_general(hi, q_lo, dn, preferred_element_type=f32)
        + lax.dot_general(lo, q_hi, dn, preferred_element_type=f32)
    )


def cosine_forward(v):
    n = len(v)
    if n == 1:
        return [v[0]]
    h = n // 2
    sums = [v[z] + v[n - 1 - z] for z in range(h)]
    diffs = [v[z] - v[n - 1 - z] for z in range(h)]
    even = cosine_forward(sums)
    out = [None] * n
    for j in range(h):
        out[2 * j] = even[j]
        k = 2 * j + 1
        acc = None
        for z in range(h):
            term = diffs[z] * float(math.cos(math.pi * k * (z + 0.5) / n))
            acc = term if acc is None else acc + term
        out[k] = acc
    return out


def cosine_backward(c):
    n = len(c)
    if n == 1:
        return [c[0]]
    h = n // 2
    even = cosine_backward([c[2 * j] for j in range(h)])
    out = [None] * n
    for z in range(h):
        acc = None
        for j in range(h):
            k = 2 * j + 1
            term = c[k] * float(math.cos(math.pi * k * (z + 0.5) / n))
            acc = term if acc is None else acc + term
        out[z] = even[z] + acc
        out[n - 1 - z] = even[z] - acc
    return out


def line_factors(eig_rows, spread, layer_eig):
    rest = 1.0 + spread * (eig_rows + layer_eig)
    root = jnp.sqrt(rest * (rest + 4.0 * spread))
    decay = 2.0 * spread / (rest + 2.0 * spread + root)
    return decay, root


def power(base, exponent):
    out = None
    square = base
    while exponent:
        if exponent & 1:
            out = square if out is None else out * square
        exponent >>= 1
        if exponent:
            square = square * square
    return out


def sublane_powers(step_decay, row, reverse):
    out = jnp.ones_like(step_decay)
    factor = step_decay
    place = (SUB - 1 - row) if reverse else row
    for bit in range(3):
        out = jnp.where((place >> bit) & 1 == 1, out * factor, out)
        factor = factor * factor
    return out


def on_device_fn(fields, grain_ids, grain_rates, die_mask):
    depth = fields.shape[1]
    local_x = fields.shape[2]
    span_y = fields.shape[3]
    half = span_y // 2
    devices_x = lax.axis_size("gx")
    devices_z = lax.axis_size("gz")
    layers = depth * devices_z
    chunks = devices_z // 2
    lanes = span_y // chunks
    steps = local_x // SUB
    tiles = span_y // LANES
    grain_count = grain_rates.shape[0]
    even, odd, eig = split_tables(span_y)
    even_hi, even_lo = table_pair(even)
    odd_hi, odd_lo = table_pair(odd)
    tables = [jnp.asarray(t) for t in (even_hi, even_lo, odd_hi, odd_lo)]
    back_tables = [jnp.asarray(np.ascontiguousarray(t.T)) for t in (even_hi, even_lo, odd_hi, odd_lo)]
    eig_table = jnp.asarray(eig.reshape(chunks, lanes))
    f32 = jnp.float32
    cover = pl.CostEstimate(flops=8 * 10**9, transcendentals=0, bytes_accessed=24 * 10**6)
    params = pltpu.CompilerParams(vmem_limit_bytes=VMEM_LIMIT)
    piece = (depth, steps, SUB, lanes)
    grain_run = min(steps, 8)
    mask_run = min(steps, 16)

    vmem = pl.BlockSpec(memory_space=pltpu.VMEM)
    hbm = pl.BlockSpec(memory_space=pltpu.HBM)
    shared = 2 if depth % 2 == 0 else 1

    grain_runs = max(steps // 8, 1)
    mask_runs = max(steps // 16, 1)
    ahead = (
        jax.ShapeDtypeStruct((depth, tiles, 2, local_x, LANES), f32),
        jax.ShapeDtypeStruct((2, depth // shared, tiles, grain_runs, SUB, LANES), f32),
        jax.ShapeDtypeStruct((tiles, mask_runs, SUB, LANES), f32),
    ) + tuple(jax.ShapeDtypeStruct((half, half), jnp.bfloat16) for _ in range(4))

    def fill(heat, tile, f_buf, rate_buf, sink_buf, sums, diffs):
        for xi in range(steps):
            at = pl.ds(xi, SUB, stride=steps)
            for layer in range(depth):
                rhs = []
                for t in (tile, tile + tiles // 2):
                    rate = rate_buf[int(heat), layer // shared, t, xi // 8]
                    c = f_buf[layer, t, 0, at, :]
                    h = f_buf[layer, t, 1, at, :]
                    if heat:
                        c2 = c * c
                        value = h + rate * c2 / (1.0 + c2)
                        if layer == 0:
                            value = value - sink_buf[t, xi // 16] * (h + 1.0)
                    else:
                        value = c + rate * jnp.tanh(h - c)
                    rhs.append(value)
                rows = pl.ds((layer * steps + xi) * SUB, SUB)
                cols = pl.ds(tile * LANES, LANES)
                sums[rows, cols] = rhs[0] + rhs[1]
                diffs[rows, cols] = rhs[0] - rhs[1]

    def forward_y(g, tables_y, sums, diffs, modes, outs):
        eh, el, oh, ol = tables_y
        for parity, (src, hi, lo) in enumerate(((sums, eh, el), (diffs, oh, ol))):
            both = dot3(src[...], hi[...], lo[...], ((1,), (0,)))
            for chunk in range(chunks // 2):
                part = both[:, chunk * lanes : (chunk + 1) * lanes]
                modes[parity * (chunks // 2) + chunk] = part.reshape(piece)
        for j in range(chunks):
            outs[j][...] = modes[(g // 2) ^ j]

    def first_kernel(rates_hbm, f_hbm, id_hbm, mask_hbm, *rest):
        tables_hbm, outs = rest[:4], rest[4 : 4 + chunks]
        f_buf, rate_buf, sink_buf = rest[4 + chunks : 7 + chunks]
        tables_y = rest[7 + chunks : 11 + chunks]
        id_buf, mask_buf, sums, diffs, modes, rates = rest[11 + chunks : -4]
        f_sems, id_sems, mask_sems, table_sems = rest[-4:]
        g = lax.axis_index("gz")
        field = g % 2
        rate_copy = pltpu.make_async_copy(rates_hbm, rates, table_sems.at[4])
        id_copies = [
            [
                pltpu.make_async_copy(
                    id_hbm.at[group * shared, :, pl.ds(t * LANES, LANES)],
                    id_buf.at[group, t],
                    id_sems.at[group, t],
                )
                for group in range(depth // shared)
            ]
            for t in range(tiles)
        ]
        mask_copies = [
            pltpu.make_async_copy(
                mask_hbm.at[:, pl.ds(t * LANES, LANES)], mask_buf.at[t], mask_sems.at[t]
            )
            for t in range(tiles)
        ]
        field_copies = [
            [
                pltpu.make_async_copy(
                    f_hbm.at[:, layer, :, pl.ds(t * LANES, LANES)],
                    f_buf.at[layer, t],
                    f_sems.at[layer, t],
                )
                for layer in range(depth)
            ]
            for t in range(tiles)
        ]
        table_copies = [
            pltpu.make_async_copy(tables_hbm[i], tables_y[i], table_sems.at[i]) for i in range(4)
        ]
        rate_copy.start()
        for copies in id_copies:
            for copy in copies:
                copy.start()

        @pl.when(g == 0)
        def _():
            for copy in mask_copies:
                copy.start()

        for tile in range(tiles // 2):
            for t in (tile, tile + tiles // 2):
                for copy in field_copies[t]:
                    copy.start()
        for copy in table_copies:
            copy.start()
        rate_copy.wait()
        for copies in id_copies:
            for copy in copies:
                copy.wait()
        for group in range(depth // shared):
            for t in range(tiles):
                for run in range(grain_runs):
                    ids = id_buf[group, t, pl.ds(run * 8, SUB, stride=steps), :]
                    found = [jnp.zeros(ids.shape, f32)] * 2
                    for grain in range(grain_count):
                        hit = ids == grain
                        found = [jnp.where(hit, rates[f, grain], found[f]) for f in range(2)]
                    for f in range(2):
                        rate_buf[f, group, t, run] = found[f]

        @pl.when(g == 0)
        def _():
            for copy in mask_copies:
                copy.wait()
            for t in range(tiles):
                for run in range(mask_runs):
                    mask = mask_buf[t, pl.ds(run * 16, SUB, stride=steps), :]
                    sink_buf[t, run] = mask.astype(f32) * heat_loss

        @pl.when(g != 0)
        def _():
            sink_buf[...] = jnp.zeros_like(sink_buf)

        for tile in range(tiles // 2):
            for t in (tile, tile + tiles // 2):
                for copy in field_copies[t]:
                    copy.wait()
            for heat in (False, True):
                pl.when(field == int(heat))(
                    functools.partial(fill, heat, tile, f_buf, rate_buf, sink_buf, sums, diffs)
                )
        for copy in table_copies:
            copy.wait()
        forward_y(g, tables_y, sums, diffs, modes, outs)

    def second_kernel(f_buf, rate_buf, sink_buf, *rest):
        tables_y, outs = rest[:4], rest[4 : 4 + chunks]
        sums, diffs, modes = rest[4 + chunks :]
        g = lax.axis_index("gz")
        for heat in (False, True):

            @pl.when(1 - g % 2 == int(heat))
            def _(heat=heat):
                for tile in range(tiles // 2):
                    fill(heat, tile, f_buf, rate_buf, sink_buf, sums, diffs)

        forward_y(g, tables_y, sums, diffs, modes, outs)

    piece_shapes = [jax.ShapeDtypeStruct(piece, f32)] * chunks
    work_scratch = [
        pltpu.VMEM((depth * local_x, half), f32),
        pltpu.VMEM((depth * local_x, half), f32),
        pltpu.VMEM((chunks,) + piece, f32),
    ]
    first_out = pl.pallas_call(
        first_kernel,
        in_specs=[hbm] * 8,
        out_specs=[vmem] * (chunks + len(ahead)),
        out_shape=piece_shapes + list(ahead),
        scratch_shapes=[
            pltpu.VMEM((depth // shared, tiles, local_x, LANES), jnp.int32),
            pltpu.VMEM((tiles, local_x, LANES), jnp.int32),
            *work_scratch,
            pltpu.SMEM((2, grain_count), f32),
            pltpu.SemaphoreType.DMA((depth, tiles)),
            pltpu.SemaphoreType.DMA((depth // shared, tiles)),
            pltpu.SemaphoreType.DMA((tiles,)),
            pltpu.SemaphoreType.DMA((5,)),
        ],
        compiler_params=params,
        name="sources_own",
    )(
        *(
            pltpu.with_memory_space_constraint(a, pltpu.HBM)
            for a in (grain_rates.T, fields, grain_ids, die_mask, *tables)
        )
    )
    own_pieces = first_out[:chunks]
    other_pieces = pl.pallas_call(
        second_kernel,
        in_specs=[vmem] * len(ahead),
        out_specs=[vmem] * chunks,
        out_shape=piece_shapes,
        scratch_shapes=work_scratch,
        compiler_params=params,
        cost_estimate=cover,
        name="sources_other",
    )(*first_out[chunks:])
    pieces = [(own_pieces, other_pieces)[k % 2][k // 2] for k in range(devices_z)]

    def exchange(arrays, axis, order):
        count = lax.axis_size(axis)
        out = []
        for k in order:
            route = [(i, i ^ k) for i in range(count)]
            out.append(lax.ppermute(arrays[k], axis, route) if k else arrays[k])
        return out

    order_own = [0] + list(range(1, chunks))[::-1]
    order_other = list(range(chunks))[::-1]
    order_z = [2 * j for j in order_own] + [2 * j + 1 for j in order_other]
    order_x = list(range(devices_x))

    gathered = exchange(pieces, "gz", order_z)

    def line_setup(eig_ref):
        g = lax.axis_index("gz")
        spread = jnp.where(g % 2 == 0, spread_solute, spread_heat).astype(f32)
        eig_rows = jnp.broadcast_to(eig_ref[pl.ds(g // 2, 1), :], (SUB, lanes))
        return g, spread, eig_rows

    layer_eig = [4.0 * math.sin(math.pi * k / (2 * layers)) ** 2 for k in range(layers)]

    def gather_kernel(eig_ref, *rest):
        ins = rest[: devices_z]
        hat_ref, from_left, from_right, ends, field = rest[devices_z:]
        g, spread, eig_rows = line_setup(eig_ref)
        for i, k in enumerate(order_z):
            field[pl.ds((g ^ k) * depth, depth)] = ins[i][...]

        def transform(xi, carry):
            hat = cosine_forward([field[z, xi] for z in range(layers)])
            for k in range(layers):
                hat_ref[k, xi] = hat[k]
            return carry

        lax.fori_loop(0, steps, transform, 0)
        row = lax.broadcasted_iota(jnp.int32, (SUB, lanes), 0)
        for k in range(layers):
            decay, _ = line_factors(eig_rows, spread, layer_eig[k])
            left = hat_ref[k, 0]
            right = hat_ref[k, steps - 1]
            for xi in range(1, steps):
                left = hat_ref[k, xi] + decay * left
                right = hat_ref[k, steps - 1 - xi] + decay * right
            step_decay = power(decay, steps)
            up = sublane_powers(step_decay, row, False)
            down = sublane_powers(step_decay, row, True)
            ends[0, pl.ds(k, 1), :] = jnp.sum(left * down, axis=0, keepdims=True)
            ends[1, pl.ds(k, 1), :] = jnp.sum(right * up, axis=0, keepdims=True)
            left = jnp.where(row >= 1, pltpu.roll(left, 1, 0), 0.0)
            right = jnp.where(row < SUB - 1, pltpu.roll(right, SUB - 1, 0), 0.0)
            factor = step_decay
            for shift in (1, 2, 4):
                left = left + factor * jnp.where(row >= shift, pltpu.roll(left, shift, 0), 0.0)
                right = right + factor * jnp.where(
                    row < SUB - shift, pltpu.roll(right, SUB - shift, 0), 0.0
                )
                factor = factor * factor
            from_left[k] = left
            from_right[k] = right

    hat, from_left, from_right, ends = pl.pallas_call(
        gather_kernel,
        in_specs=[vmem] * (1 + devices_z),
        out_specs=[vmem] * 4,
        out_shape=[
            jax.ShapeDtypeStruct((layers, steps, SUB, lanes), f32),
            jax.ShapeDtypeStruct((layers, SUB, lanes), f32),
            jax.ShapeDtypeStruct((layers, SUB, lanes), f32),
            jax.ShapeDtypeStruct((2, layers, lanes), f32),
        ],
        scratch_shapes=[
            pltpu.VMEM((layers, steps, SUB, lanes), f32),
        ],
        compiler_params=params,
        name="gather",
    )(eig_table, *gathered)

    all_ends = exchange([ends] * devices_x, "gx", order_x)

    def solve_kernel(eig_ref, hat_ref, left_ref, right_ref, *rest):
        end_refs = rest[: devices_x]
        outs = rest[devices_x : devices_x + devices_z]
        near, work, entry = rest[devices_x + devices_z :]
        g, spread, eig_rows = line_setup(eig_ref)
        place = lax.axis_index("gx")
        for i, k in enumerate(order_x):
            near[place ^ k] = end_refs[i][...]
        row = lax.broadcasted_iota(jnp.int32, (SUB, lanes), 0)
        eig_one = eig_ref[pl.ds(g // 2, 1), :]
        kz = lax.broadcasted_iota(jnp.int32, (layers, lanes), 0).astype(f32)
        eig_z = 4.0 * jnp.sin(kz * (math.pi / (2 * layers))) ** 2
        decay_all, _ = line_factors(eig_one, spread, eig_z)
        block_decay = power(decay_all, local_x)
        total_left = near[(place + devices_x - 1) % devices_x, 0]
        total_right = near[(place + 1) % devices_x, 1]
        weight = block_decay
        for m in range(2, devices_x + 1):
            total_left = total_left + weight * near[(place + devices_x - m) % devices_x, 0]
            total_right = total_right + weight * near[(place + m) % devices_x, 1]
            weight = weight * block_decay
        entry[0] = total_left / (1.0 - weight)
        entry[1] = total_right / (1.0 - weight)
        for k in range(layers):
            decay, root = line_factors(eig_rows, spread, layer_eig[k])
            gain = ((1.0 if k == 0 else 2.0) / layers) / root
            step_decay = power(decay, steps)
            up = sublane_powers(step_decay, row, False)
            down = sublane_powers(step_decay, row, True)
            left = left_ref[k] + up * entry[0, pl.ds(k, 1), :]
            right = right_ref[k] + down * entry[1, pl.ds(k, 1), :]
            for xi in range(steps):
                left = hat_ref[k, xi] + decay * left
                work[k, xi] = left
            for xi in reversed(range(steps)):
                carried = decay * right
                work[k, xi] = gain * (work[k, xi] + carried)
                right = hat_ref[k, xi] + carried

        def back(xi, carry):
            values = cosine_backward([work[k, xi] for k in range(layers)])
            for z in range(layers):
                work[z, xi] = values[z]
            return carry

        lax.fori_loop(0, steps, back, 0)
        for k in range(devices_z):
            outs[k][...] = work[pl.ds((g ^ k) * depth, depth)]

    solved = pl.pallas_call(
        solve_kernel,
        in_specs=[vmem] * (4 + devices_x),
        out_specs=[vmem] * devices_z,
        out_shape=[jax.ShapeDtypeStruct(piece, f32)] * devices_z,
        scratch_shapes=[
            pltpu.VMEM((devices_x, 2, layers, lanes), f32),
            pltpu.VMEM((layers, steps, SUB, lanes), f32),
            pltpu.VMEM((2, layers, lanes), f32),
        ],
        compiler_params=params,
        name="solve",
    )(eig_table, hat, from_left, from_right, *all_ends)

    returned = exchange(solved, "gz", order_z)

    def backward_y(tables_y, order, ins, modes, buf, done):
        eh, el, oh, ol = tables_y
        g = lax.axis_index("gz")
        for i, j in enumerate(order):
            modes[(g // 2) ^ j] = ins[i][...]
        dims = ((1,), (0,))
        parts = [modes[chunk].reshape(depth * local_x, lanes) for chunk in range(chunks)]
        low = dot3(jnp.concatenate(parts[: chunks // 2], axis=1), eh[...], el[...], dims)
        high = dot3(jnp.concatenate(parts[chunks // 2 :], axis=1), oh[...], ol[...], dims)
        for side, value in enumerate((low + high, low - high)):
            for layer in range(depth):
                for col in range(tiles // 2):
                    t = side * (tiles // 2) + col
                    for xi in range(steps):
                        at = (layer * steps + xi) * SUB
                        buf[layer, t, pl.ds(xi, SUB, stride=steps), :] = value[
                            at : at + SUB, col * LANES : (col + 1) * LANES
                        ]
                    done(layer, t)

    def own_kernel(*refs):
        buf, modes = refs[4 + chunks :]
        backward_y(refs[:4], order_own, refs[4 : 4 + chunks], modes, buf, lambda layer, t: None)

    def other_kernel(own_buf, *refs):
        out_ref, modes, buf, own_sems, sems = refs[4 + chunks :]
        mine = lax.axis_index("gz") % 2
        copies = []

        def send(source, field, layer, t, sem):
            copies.append(
                pltpu.make_async_copy(
                    source.at[layer, t], out_ref.at[field, layer, :, pl.ds(t * LANES, LANES)], sem
                )
            )
            copies[-1].start()

        for layer in range(depth):
            for t in range(tiles):
                send(own_buf, mine, layer, t, own_sems.at[layer, t])
        backward_y(
            refs[:4],
            order_other,
            refs[4 : 4 + chunks],
            modes,
            buf,
            lambda layer, t: send(buf, 1 - mine, layer, t, sems.at[layer, t]),
        )
        for copy in copies:
            copy.wait()

    by_source = dict(zip(order_z, returned))
    buffer = (depth, tiles, local_x, LANES)
    modes_scratch = pltpu.VMEM((chunks,) + piece, f32)
    own_buf = pl.pallas_call(
        own_kernel,
        in_specs=[vmem] * (4 + chunks),
        out_specs=vmem,
        out_shape=jax.ShapeDtypeStruct(buffer, f32),
        scratch_shapes=[modes_scratch],
        compiler_params=params,
        cost_estimate=cover,
        name="finish_own",
    )(*back_tables, *(by_source[2 * j] for j in order_own))
    tile_sems = pltpu.SemaphoreType.DMA((depth, tiles))
    return pl.pallas_call(
        other_kernel,
        in_specs=[vmem] * (5 + chunks),
        out_specs=hbm,
        out_shape=jax.ShapeDtypeStruct((2, depth, local_x, span_y), f32),
        scratch_shapes=[modes_scratch, pltpu.VMEM(buffer, f32), tile_sems, tile_sems],
        compiler_params=params,
        name="finish_other",
    )(own_buf, *back_tables, *(by_source[2 * j + 1] for j in order_other))


def solution(mesh):
    placed = (P(None, "gz", "gx", None), P("gz", "gx", None), P(), P("gx", None))
    return jax.shard_map(
        on_device_fn, mesh=mesh, in_specs=placed, out_specs=P(None, "gz", "gx", None), check_vma=False
    )
```

```python
import functools
import math

import numpy as np
import jax
import jax.numpy as jnp
from jax import lax
from jax.experimental import pallas as pl
from jax.experimental.pallas import tpu as pltpu
from jax.sharding import PartitionSpec as P

heat_loss = 4.0
spread_solute = 2.0
spread_heat = 100.0
SUB = 8
LANES = 128
VMEM_LIMIT = 48 * 1024 * 1024


def split_tables(n):
    half = n // 2
    y = np.arange(half)
    cols, freq = [], []
    for j in range(half // 2 + 1):
        k = 2 * j
        scale = math.sqrt((1.0 if k in (0, half) else 2.0) / n)
        cols.append(scale * np.cos(2 * np.pi * k * y / n))
        freq.append(k)
        if 0 < j < half // 2:
            cols.append(scale * np.sin(2 * np.pi * k * y / n))
            freq.append(k)
    even = np.stack(cols, 1)
    cols, odd_freq = [], []
    for j in range(half // 2):
        k = 2 * j + 1
        scale = math.sqrt(2.0 / n)
        cols.append(scale * np.cos(2 * np.pi * k * y / n))
        cols.append(scale * np.sin(2 * np.pi * k * y / n))
        odd_freq += [k, k]
    odd = np.stack(cols, 1)
    eig = 4.0 * np.sin(np.pi * np.array(freq + odd_freq) / n) ** 2
    return even, odd, eig.astype(np.float32)


def hi_lo(a):
    hi = jnp.asarray(a, jnp.float32).astype(jnp.bfloat16)
    lo = (jnp.asarray(a, jnp.float32) - hi.astype(jnp.float32)).astype(jnp.bfloat16)
    return hi, lo


def table_pair(a):
    bf16 = jnp.bfloat16
    hi = a.astype(np.float32).astype(bf16)
    lo = (a - hi.astype(np.float64)).astype(np.float32).astype(bf16)
    return hi, lo


def dot3(x, q_hi, q_lo, dims):
    hi, lo = hi_lo(x)
    dn = (dims, ((), ()))
    f32 = jnp.float32
    return (
        lax.dot_general(hi, q_hi, dn, preferred_element_type=f32)
        + lax.dot_general(hi, q_lo, dn, preferred_element_type=f32)
        + lax.dot_general(lo, q_hi, dn, preferred_element_type=f32)
    )


def cosine_forward(v):
    n = len(v)
    if n == 1:
        return [v[0]]
    h = n // 2
    sums = [v[z] + v[n - 1 - z] for z in range(h)]
    diffs = [v[z] - v[n - 1 - z] for z in range(h)]
    even = cosine_forward(sums)
    out = [None] * n
    for j in range(h):
        out[2 * j] = even[j]
        k = 2 * j + 1
        acc = None
        for z in range(h):
            term = diffs[z] * float(math.cos(math.pi * k * (z + 0.5) / n))
            acc = term if acc is None else acc + term
        out[k] = acc
    return out


def cosine_backward(c):
    n = len(c)
    if n == 1:
        return [c[0]]
    h = n // 2
    even = cosine_backward([c[2 * j] for j in range(h)])
    out = [None] * n
    for z in range(h):
        acc = None
        for j in range(h):
            k = 2 * j + 1
            term = c[k] * float(math.cos(math.pi * k * (z + 0.5) / n))
            acc = term if acc is None else acc + term
        out[z] = even[z] + acc
        out[n - 1 - z] = even[z] - acc
    return out


def line_factors(eig_rows, spread, layer_eig):
    rest = 1.0 + spread * (eig_rows + layer_eig)
    root = jnp.sqrt(rest * (rest + 4.0 * spread))
    decay = 2.0 * spread / (rest + 2.0 * spread + root)
    return decay, root


def power(base, exponent):
    out = None
    square = base
    while exponent:
        if exponent & 1:
            out = square if out is None else out * square
        exponent >>= 1
        if exponent:
            square = square * square
    return out


def sublane_powers(step_decay, row, reverse):
    out = jnp.ones_like(step_decay)
    factor = step_decay
    place = (SUB - 1 - row) if reverse else row
    for bit in range(3):
        out = jnp.where((place >> bit) & 1 == 1, out * factor, out)
        factor = factor * factor
    return out


def on_device_fn(fields, grain_ids, grain_rates, die_mask):
    depth = fields.shape[1]
    local_x = fields.shape[2]
    span_y = fields.shape[3]
    half = span_y // 2
    devices_x = lax.axis_size("gx")
    devices_z = lax.axis_size("gz")
    layers = depth * devices_z
    chunks = devices_z // 2
    lanes = span_y // chunks
    steps = local_x // SUB
    tiles = span_y // LANES
    grain_count = grain_rates.shape[0]
    even, odd, eig = split_tables(span_y)
    even_hi, even_lo = table_pair(even)
    odd_hi, odd_lo = table_pair(odd)
    tables = [jnp.asarray(t) for t in (even_hi, even_lo, odd_hi, odd_lo)]
    back_tables = [jnp.asarray(np.ascontiguousarray(t.T)) for t in (even_hi, even_lo, odd_hi, odd_lo)]
    eig_table = jnp.asarray(eig.reshape(chunks, lanes))
    f32 = jnp.float32
    cover = pl.CostEstimate(flops=8 * 10**9, transcendentals=0, bytes_accessed=24 * 10**6)
    params = pltpu.CompilerParams(vmem_limit_bytes=VMEM_LIMIT)
    piece = (depth, steps, SUB, lanes)
    grain_run = min(steps, 8)
    mask_run = min(steps, 16)

    vmem = pl.BlockSpec(memory_space=pltpu.VMEM)
    hbm = pl.BlockSpec(memory_space=pltpu.HBM)
    shared = 2 if depth % 2 == 0 else 1

    grain_runs = max(steps // 8, 1)
    mask_runs = max(steps // 16, 1)
    ahead = (
        jax.ShapeDtypeStruct((depth, tiles, 2, local_x, LANES), f32),
        jax.ShapeDtypeStruct((2, depth // shared, tiles, grain_runs, SUB, LANES), f32),
        jax.ShapeDtypeStruct((tiles, mask_runs, SUB, LANES), f32),
    ) + tuple(jax.ShapeDtypeStruct((half, half), jnp.bfloat16) for _ in range(4))

    layer_eig = [4.0 * math.sin(math.pi * k / (2 * layers)) ** 2 for k in range(layers)]
    per_run = jax.ShapeDtypeStruct((layers, SUB, lanes), f32)
    factor_shapes = [per_run] * 4 + [jax.ShapeDtypeStruct((devices_x, layers, lanes), f32)]

    def fill(heat, tile, f_buf, rate_buf, sink_buf, sums, diffs):
        for xi in range(steps):
            at = pl.ds(xi, SUB, stride=steps)
            for layer in range(depth):
                rhs = []
                for t in (tile, tile + tiles // 2):
                    rate = rate_buf[int(heat), layer // shared, t, xi // 8]
                    c = f_buf[layer, t, 0, at, :]
                    h = f_buf[layer, t, 1, at, :]
                    if heat:
                        c2 = c * c
                        value = h + rate * c2 / (1.0 + c2)
                        if layer == 0:
                            value = value - sink_buf[t, xi // 16] * (h + 1.0)
                    else:
                        value = c + rate * jnp.tanh(h - c)
                    rhs.append(value)
                rows = pl.ds((layer * steps + xi) * SUB, SUB)
                cols = pl.ds(tile * LANES, LANES)
                sums[rows, cols] = rhs[0] + rhs[1]
                diffs[rows, cols] = rhs[0] - rhs[1]

    def forward_y(g, tables_y, sums, diffs, modes, outs):
        eh, el, oh, ol = tables_y
        for parity, (src, hi, lo) in enumerate(((sums, eh, el), (diffs, oh, ol))):
            both = dot3(src[...], hi[...], lo[...], ((1,), (0,)))
            for chunk in range(chunks // 2):
                part = both[:, chunk * lanes : (chunk + 1) * lanes]
                modes[parity * (chunks // 2) + chunk] = part.reshape(piece)
        for j in range(chunks):
            outs[j][...] = modes[(g // 2) ^ j]

    def first_kernel(rates_hbm, eig_hbm, f_hbm, id_hbm, mask_hbm, *rest):
        tables_hbm, outs = rest[:4], rest[4 : 4 + chunks]
        f_buf, rate_buf, sink_buf = rest[4 + chunks : 7 + chunks]
        tables_y = rest[7 + chunks : 11 + chunks]
        decay_ref, gain_ref, up_ref, down_ref, weight_ref = rest[11 + chunks : 16 + chunks]
        id_buf, mask_buf, sums, diffs, modes, rates, eig_ref = rest[16 + chunks : -4]
        f_sems, id_sems, mask_sems, table_sems = rest[-4:]
        g = lax.axis_index("gz")
        field = g % 2
        rate_copy = pltpu.make_async_copy(rates_hbm, rates, table_sems.at[4])
        id_copies = [
            [
                pltpu.make_async_copy(
                    id_hbm.at[group * shared, :, pl.ds(t * LANES, LANES)],
                    id_buf.at[group, t],
                    id_sems.at[group, t],
                )
                for group in range(depth // shared)
            ]
            for t in range(tiles)
        ]
        mask_copies = [
            pltpu.make_async_copy(
                mask_hbm.at[:, pl.ds(t * LANES, LANES)], mask_buf.at[t], mask_sems.at[t]
            )
            for t in range(tiles)
        ]
        field_copies = [
            [
                pltpu.make_async_copy(
                    f_hbm.at[:, layer, :, pl.ds(t * LANES, LANES)],
                    f_buf.at[layer, t],
                    f_sems.at[layer, t],
                )
                for layer in range(depth)
            ]
            for t in range(tiles)
        ]
        table_copies = [
            pltpu.make_async_copy(tables_hbm[i], tables_y[i], table_sems.at[i]) for i in range(4)
        ]
        eig_copy = pltpu.make_async_copy(eig_hbm, eig_ref, table_sems.at[5])
        eig_copy.start()
        rate_copy.start()
        for copies in id_copies:
            for copy in copies:
                copy.start()

        @pl.when(g == 0)
        def _():
            for copy in mask_copies:
                copy.start()

        for tile in range(tiles // 2):
            for t in (tile, tile + tiles // 2):
                for copy in field_copies[t]:
                    copy.start()
        for copy in table_copies:
            copy.start()
        eig_copy.wait()
        spread = jnp.where(g % 2 == 0, spread_solute, spread_heat).astype(f32)
        eig_one = eig_ref[pl.ds(g // 2, 1), :]
        eig_rows = jnp.broadcast_to(eig_one, (SUB, lanes))
        row = lax.broadcasted_iota(jnp.int32, (SUB, lanes), 0)
        for k in range(layers):
            decay, root = line_factors(eig_rows, spread, layer_eig[k])
            step_decay = power(decay, steps)
            decay_ref[k] = decay
            gain_ref[k] = ((1.0 if k == 0 else 2.0) / layers) / root
            up_ref[k] = sublane_powers(step_decay, row, False)
            down_ref[k] = sublane_powers(step_decay, row, True)
            block_decay = power(decay[:1], local_x)
            weight = jnp.ones_like(block_decay)
            for m in range(devices_x):
                weight_ref[m, pl.ds(k, 1), :] = weight
                weight = weight * block_decay
            for m in range(devices_x):
                weight_ref[m, pl.ds(k, 1), :] = weight_ref[m, pl.ds(k, 1), :] / (1.0 - weight)
        rate_copy.wait()
        for copies in id_copies:
            for copy in copies:
                copy.wait()
        for group in range(depth // shared):
            for t in range(tiles):
                for run in range(grain_runs):
                    ids = id_buf[group, t, pl.ds(run * 8, SUB, stride=steps), :]
                    found = [jnp.zeros(ids.shape, f32)] * 2
                    for grain in range(grain_count):
                        hit = ids == grain
                        found = [jnp.where(hit, rates[f, grain], found[f]) for f in range(2)]
                    for f in range(2):
                        rate_buf[f, group, t, run] = found[f]

        @pl.when(g == 0)
        def _():
            for copy in mask_copies:
                copy.wait()
            for t in range(tiles):
                for run in range(mask_runs):
                    mask = mask_buf[t, pl.ds(run * 16, SUB, stride=steps), :]
                    sink_buf[t, run] = mask.astype(f32) * heat_loss

        @pl.when(g != 0)
        def _():
            sink_buf[...] = jnp.zeros_like(sink_buf)

        for tile in range(tiles // 2):
            for t in (tile, tile + tiles // 2):
                for copy in field_copies[t]:
                    copy.wait()
            for heat in (False, True):
                pl.when(field == int(heat))(
                    functools.partial(fill, heat, tile, f_buf, rate_buf, sink_buf, sums, diffs)
                )
        for copy in table_copies:
            copy.wait()
        forward_y(g, tables_y, sums, diffs, modes, outs)

    def second_kernel(f_buf, rate_buf, sink_buf, *rest):
        tables_y, outs = rest[:4], rest[4 : 4 + chunks]
        sums, diffs, modes = rest[4 + chunks :]
        g = lax.axis_index("gz")
        for heat in (False, True):

            @pl.when(1 - g % 2 == int(heat))
            def _(heat=heat):
                for tile in range(tiles // 2):
                    fill(heat, tile, f_buf, rate_buf, sink_buf, sums, diffs)

        forward_y(g, tables_y, sums, diffs, modes, outs)

    piece_shapes = [jax.ShapeDtypeStruct(piece, f32)] * chunks
    work_scratch = [
        pltpu.VMEM((depth * local_x, half), f32),
        pltpu.VMEM((depth * local_x, half), f32),
        pltpu.VMEM((chunks,) + piece, f32),
    ]
    first_out = pl.pallas_call(
        first_kernel,
        in_specs=[hbm] * 9,
        out_specs=[vmem] * (chunks + len(ahead) + len(factor_shapes)),
        out_shape=piece_shapes + list(ahead) + factor_shapes,
        scratch_shapes=[
            pltpu.VMEM((depth // shared, tiles, local_x, LANES), jnp.int32),
            pltpu.VMEM((tiles, local_x, LANES), jnp.int32),
            *work_scratch,
            pltpu.SMEM((2, grain_count), f32),
            pltpu.VMEM((chunks, lanes), f32),
            pltpu.SemaphoreType.DMA((depth, tiles)),
            pltpu.SemaphoreType.DMA((depth // shared, tiles)),
            pltpu.SemaphoreType.DMA((tiles,)),
            pltpu.SemaphoreType.DMA((6,)),
        ],
        compiler_params=params,
        name="sources_own",
    )(
        *(
            pltpu.with_memory_space_constraint(a, pltpu.HBM)
            for a in (grain_rates.T, eig_table, fields, grain_ids, die_mask, *tables)
        )
    )
    own_pieces = first_out[:chunks]
    other_pieces = pl.pallas_call(
        second_kernel,
        in_specs=[vmem] * len(ahead),
        out_specs=[vmem] * chunks,
        out_shape=piece_shapes,
        scratch_shapes=work_scratch,
        compiler_params=params,
        cost_estimate=cover,
        name="sources_other",
    )(*first_out[chunks : chunks + len(ahead)])
    decays, gains, ups, downs, weights = first_out[chunks + len(ahead) :]
    pieces = [(own_pieces, other_pieces)[k % 2][k // 2] for k in range(devices_z)]

    def exchange(arrays, axis, order):
        count = lax.axis_size(axis)
        out = []
        for k in order:
            route = [(i, i ^ k) for i in range(count)]
            out.append(lax.ppermute(arrays[k], axis, route) if k else arrays[k])
        return out

    order_own = [0] + list(range(1, chunks))[::-1]
    order_other = list(range(chunks))[::-1]
    order_z = [2 * j for j in order_own] + [2 * j + 1 for j in order_other]
    order_x = list(range(devices_x))

    gathered = exchange(pieces, "gz", order_z)

    def gather_kernel(decay_ref, up_ref, down_ref, *rest):
        ins = rest[:devices_z]
        hat_ref, left_ref, right_ref, ends, field = rest[devices_z:]
        g = lax.axis_index("gz")
        for i, k in enumerate(order_z):
            field[pl.ds((g ^ k) * depth, depth)] = ins[i][...]

        def transform(xi, carry):
            hat = cosine_forward([field[z, xi] for z in range(layers)])
            for k in range(layers):
                hat_ref[k, xi] = hat[k]
            return carry

        lax.fori_loop(0, steps, transform, 0, unroll=4)
        for k in range(layers):
            decay = decay_ref[k]
            left = hat_ref[k, 0]
            right = hat_ref[k, steps - 1]
            for xi in range(1, steps):
                left = hat_ref[k, xi] + decay * left
                right = hat_ref[k, steps - 1 - xi] + decay * right
            ends[0, pl.ds(k, 1), :] = jnp.sum(left * down_ref[k], axis=0, keepdims=True)
            ends[1, pl.ds(k, 1), :] = jnp.sum(right * up_ref[k], axis=0, keepdims=True)
            left_ref[k] = left
            right_ref[k] = right

    hat, lefts, rights, ends = pl.pallas_call(
        gather_kernel,
        in_specs=[vmem] * (3 + devices_z),
        out_specs=[vmem] * 4,
        out_shape=[
            jax.ShapeDtypeStruct((layers, steps, SUB, lanes), f32),
            per_run,
            per_run,
            jax.ShapeDtypeStruct((2, layers, lanes), f32),
        ],
        scratch_shapes=[pltpu.VMEM((layers, steps, SUB, lanes), f32)],
        compiler_params=params,
        name="gather",
    )(decays, ups, downs, *gathered)

    def carry_kernel(decay_ref, left_ref, right_ref, from_left, from_right):
        row = lax.broadcasted_iota(jnp.int32, (SUB, lanes), 0)
        for k in range(layers):
            factor = power(decay_ref[k], steps)
            left = jnp.where(row >= 1, pltpu.roll(left_ref[k], 1, 0), 0.0)
            right = jnp.where(row < SUB - 1, pltpu.roll(right_ref[k], SUB - 1, 0), 0.0)
            for shift in (1, 2, 4):
                left = left + factor * jnp.where(row >= shift, pltpu.roll(left, shift, 0), 0.0)
                right = right + factor * jnp.where(
                    row < SUB - shift, pltpu.roll(right, SUB - shift, 0), 0.0
                )
                factor = factor * factor
            from_left[k] = left
            from_right[k] = right

    from_left, from_right = pl.pallas_call(
        carry_kernel,
        in_specs=[vmem] * 3,
        out_specs=[vmem] * 2,
        out_shape=[per_run] * 2,
        compiler_params=params,
        cost_estimate=cover,
        name="carry",
    )(decays, lefts, rights)

    all_ends = exchange([ends] * devices_x, "gx", order_x)

    def solve_kernel(decay_ref, gain_ref, up_ref, down_ref, weight_ref, hat_ref, left_ref, right_ref, *rest):
        end_refs = rest[:devices_x]
        outs = rest[devices_x : devices_x + devices_z]
        near, work, entry = rest[devices_x + devices_z :]
        g = lax.axis_index("gz")
        place = lax.axis_index("gx")
        for i, k in enumerate(order_x):
            near[place ^ k] = end_refs[i][...]
        for direction in range(2):
            total = None
            for m in range(1, devices_x + 1):
                shift = m if direction else devices_x - m
                value = weight_ref[m - 1] * near[(place + shift) % devices_x, direction]
                total = value if total is None else total + value
            entry[direction] = total
        for k in range(layers):
            decay, gain = decay_ref[k], gain_ref[k]
            left = left_ref[k] + up_ref[k] * entry[0, pl.ds(k, 1), :]
            right = right_ref[k] + down_ref[k] * entry[1, pl.ds(k, 1), :]
            for xi in range(steps):
                left = hat_ref[k, xi] + decay * left
                work[k, xi] = left
            for xi in reversed(range(steps)):
                carried = decay * right
                work[k, xi] = gain * (work[k, xi] + carried)
                right = hat_ref[k, xi] + carried

        def back(xi, carry):
            values = cosine_backward([work[k, xi] for k in range(layers)])
            for z in range(layers):
                work[z, xi] = values[z]
            return carry

        lax.fori_loop(0, steps, back, 0, unroll=4)
        for k in range(devices_z):
            outs[k][...] = work[pl.ds((g ^ k) * depth, depth)]

    solved = pl.pallas_call(
        solve_kernel,
        in_specs=[vmem] * (8 + devices_x),
        out_specs=[vmem] * devices_z,
        out_shape=[jax.ShapeDtypeStruct(piece, f32)] * devices_z,
        scratch_shapes=[
            pltpu.VMEM((devices_x, 2, layers, lanes), f32),
            pltpu.VMEM((layers, steps, SUB, lanes), f32),
            pltpu.VMEM((2, layers, lanes), f32),
        ],
        compiler_params=params,
        name="solve",
    )(decays, gains, ups, downs, weights, hat, from_left, from_right, *all_ends)

    returned = exchange(solved, "gz", order_z)

    def backward_y(tables_y, order, ins, modes, buf, done):
        eh, el, oh, ol = tables_y
        g = lax.axis_index("gz")
        for i, j in enumerate(order):
            modes[(g // 2) ^ j] = ins[i][...]
        dims = ((1,), (0,))
        parts = [modes[chunk].reshape(depth * local_x, lanes) for chunk in range(chunks)]
        low = dot3(jnp.concatenate(parts[: chunks // 2], axis=1), eh[...], el[...], dims)
        high = dot3(jnp.concatenate(parts[chunks // 2 :], axis=1), oh[...], ol[...], dims)
        for side, value in enumerate((low + high, low - high)):
            for layer in range(depth):
                for col in range(tiles // 2):
                    t = side * (tiles // 2) + col
                    for xi in range(steps):
                        at = (layer * steps + xi) * SUB
                        buf[layer, t, pl.ds(xi, SUB, stride=steps), :] = value[
                            at : at + SUB, col * LANES : (col + 1) * LANES
                        ]
                    done(layer, t)

    def own_kernel(*refs):
        buf, modes = refs[4 + chunks :]
        backward_y(refs[:4], order_own, refs[4 : 4 + chunks], modes, buf, lambda layer, t: None)

    def other_kernel(own_buf, *refs):
        out_ref, modes, buf, own_sems, sems = refs[4 + chunks :]
        mine = lax.axis_index("gz") % 2
        copies = []

        def send(source, field, layer, t, sem):
            copies.append(
                pltpu.make_async_copy(
                    source.at[layer, t], out_ref.at[field, layer, :, pl.ds(t * LANES, LANES)], sem
                )
            )
            copies[-1].start()

        for layer in range(depth):
            for t in range(tiles):
                send(own_buf, mine, layer, t, own_sems.at[layer, t])
        backward_y(
            refs[:4],
            order_other,
            refs[4 : 4 + chunks],
            modes,
            buf,
            lambda layer, t: send(buf, 1 - mine, layer, t, sems.at[layer, t]),
        )
        for copy in copies:
            copy.wait()

    by_source = dict(zip(order_z, returned))
    buffer = (depth, tiles, local_x, LANES)
    modes_scratch = pltpu.VMEM((chunks,) + piece, f32)
    own_buf = pl.pallas_call(
        own_kernel,
        in_specs=[vmem] * (4 + chunks),
        out_specs=vmem,
        out_shape=jax.ShapeDtypeStruct(buffer, f32),
        scratch_shapes=[modes_scratch],
        compiler_params=params,
        cost_estimate=cover,
        name="finish_own",
    )(*back_tables, *(by_source[2 * j] for j in order_own))
    tile_sems = pltpu.SemaphoreType.DMA((depth, tiles))
    return pl.pallas_call(
        other_kernel,
        in_specs=[vmem] * (5 + chunks),
        out_specs=hbm,
        out_shape=jax.ShapeDtypeStruct((2, depth, local_x, span_y), f32),
        scratch_shapes=[modes_scratch, pltpu.VMEM(buffer, f32), tile_sems, tile_sems],
        compiler_params=params,
        name="finish_other",
    )(own_buf, *back_tables, *(by_source[2 * j + 1] for j in order_other))


def solution(mesh):
    placed = (P(None, "gz", "gx", None), P("gz", "gx", None), P(), P("gx", None))
    return jax.shard_map(
        on_device_fn, mesh=mesh, in_specs=placed, out_specs=P(None, "gz", "gx", None), check_vma=False
    )
```

```python
import functools
import math

import numpy as np
import jax
import jax.numpy as jnp
from jax import lax
from jax.experimental import pallas as pl
from jax.experimental.pallas import tpu as pltpu
from jax.sharding import PartitionSpec as P

heat_loss = 4.0
spread_solute = 2.0
spread_heat = 100.0
SUB = 8
LANES = 128
VMEM_LIMIT = 48 * 1024 * 1024


def split_tables(n):
    half = n // 2
    y = np.arange(half)
    cols, freq = [], []
    for j in range(half // 2 + 1):
        k = 2 * j
        scale = math.sqrt((1.0 if k in (0, half) else 2.0) / n)
        cols.append(scale * np.cos(2 * np.pi * k * y / n))
        freq.append(k)
        if 0 < j < half // 2:
            cols.append(scale * np.sin(2 * np.pi * k * y / n))
            freq.append(k)
    even = np.stack(cols, 1)
    cols, odd_freq = [], []
    for j in range(half // 2):
        k = 2 * j + 1
        scale = math.sqrt(2.0 / n)
        cols.append(scale * np.cos(2 * np.pi * k * y / n))
        cols.append(scale * np.sin(2 * np.pi * k * y / n))
        odd_freq += [k, k]
    odd = np.stack(cols, 1)
    eig = 4.0 * np.sin(np.pi * np.array(freq + odd_freq) / n) ** 2
    return even, odd, eig.astype(np.float32)


def hi_lo(a):
    hi = jnp.asarray(a, jnp.float32).astype(jnp.bfloat16)
    lo = (jnp.asarray(a, jnp.float32) - hi.astype(jnp.float32)).astype(jnp.bfloat16)
    return hi, lo


def table_pair(a):
    bf16 = jnp.bfloat16
    hi = a.astype(np.float32).astype(bf16)
    lo = (a - hi.astype(np.float64)).astype(np.float32).astype(bf16)
    return hi, lo


def dot3(x, q_hi, q_lo, dims):
    hi, lo = hi_lo(x)
    dn = (dims, ((), ()))
    f32 = jnp.float32
    return (
        lax.dot_general(hi, q_hi, dn, preferred_element_type=f32)
        + lax.dot_general(hi, q_lo, dn, preferred_element_type=f32)
        + lax.dot_general(lo, q_hi, dn, preferred_element_type=f32)
    )


def cosine_forward(v):
    n = len(v)
    if n == 1:
        return [v[0]]
    h = n // 2
    sums = [v[z] + v[n - 1 - z] for z in range(h)]
    diffs = [v[z] - v[n - 1 - z] for z in range(h)]
    even = cosine_forward(sums)
    out = [None] * n
    for j in range(h):
        out[2 * j] = even[j]
        k = 2 * j + 1
        acc = None
        for z in range(h):
            term = diffs[z] * float(math.cos(math.pi * k * (z + 0.5) / n))
            acc = term if acc is None else acc + term
        out[k] = acc
    return out


def cosine_backward(c):
    n = len(c)
    if n == 1:
        return [c[0]]
    h = n // 2
    even = cosine_backward([c[2 * j] for j in range(h)])
    out = [None] * n
    for z in range(h):
        acc = None
        for j in range(h):
            k = 2 * j + 1
            term = c[k] * float(math.cos(math.pi * k * (z + 0.5) / n))
            acc = term if acc is None else acc + term
        out[z] = even[z] + acc
        out[n - 1 - z] = even[z] - acc
    return out


def line_factors(eig_rows, spread, layer_eig):
    rest = 1.0 + spread * (eig_rows + layer_eig)
    root = jnp.sqrt(rest * (rest + 4.0 * spread))
    decay = 2.0 * spread / (rest + 2.0 * spread + root)
    return decay, root


def power(base, exponent):
    out = None
    square = base
    while exponent:
        if exponent & 1:
            out = square if out is None else out * square
        exponent >>= 1
        if exponent:
            square = square * square
    return out


def sublane_powers(step_decay, row, reverse):
    out = jnp.ones_like(step_decay)
    factor = step_decay
    place = (SUB - 1 - row) if reverse else row
    for bit in range(3):
        out = jnp.where((place >> bit) & 1 == 1, out * factor, out)
        factor = factor * factor
    return out


def on_device_fn(fields, grain_ids, grain_rates, die_mask):
    depth = fields.shape[1]
    local_x = fields.shape[2]
    span_y = fields.shape[3]
    half = span_y // 2
    devices_x = lax.axis_size("gx")
    devices_z = lax.axis_size("gz")
    layers = depth * devices_z
    chunks = devices_z // 2
    lanes = span_y // chunks
    steps = local_x // SUB
    tiles = span_y // LANES
    grain_count = grain_rates.shape[0]
    even, odd, eig = split_tables(span_y)
    even_hi, even_lo = table_pair(even)
    odd_hi, odd_lo = table_pair(odd)
    tables = [jnp.asarray(t) for t in (even_hi, even_lo, odd_hi, odd_lo)]
    back_tables = [jnp.asarray(np.ascontiguousarray(t.T)) for t in (even_hi, even_lo, odd_hi, odd_lo)]
    eig_table = jnp.asarray(eig.reshape(chunks, lanes))
    f32 = jnp.float32
    cover = pl.CostEstimate(flops=8 * 10**9, transcendentals=0, bytes_accessed=24 * 10**6)
    params = pltpu.CompilerParams(vmem_limit_bytes=VMEM_LIMIT)
    piece = (depth, steps, SUB, lanes)
    grain_run = min(steps, 8)
    mask_run = min(steps, 16)

    vmem = pl.BlockSpec(memory_space=pltpu.VMEM)
    hbm = pl.BlockSpec(memory_space=pltpu.HBM)
    shared = 2 if depth % 2 == 0 else 1

    grain_runs = max(steps // 8, 1)
    mask_runs = max(steps // 16, 1)
    ahead = (
        jax.ShapeDtypeStruct((depth, tiles, 2, local_x, LANES), f32),
        jax.ShapeDtypeStruct((2, depth // shared, tiles, grain_runs, SUB, LANES), f32),
        jax.ShapeDtypeStruct((tiles, mask_runs, SUB, LANES), f32),
    ) + tuple(jax.ShapeDtypeStruct((half, half), jnp.bfloat16) for _ in range(4))

    layer_eig = [4.0 * math.sin(math.pi * k / (2 * layers)) ** 2 for k in range(layers)]
    per_run = jax.ShapeDtypeStruct((layers, SUB, lanes), f32)
    factor_shapes = [per_run] * 4 + [jax.ShapeDtypeStruct((devices_x, layers, lanes), f32)]

    def fill(heat, tile, f_buf, rate_buf, sink_buf, sums, diffs):
        for xi in range(steps):
            at = pl.ds(xi, SUB, stride=steps)
            for layer in range(depth):
                rhs = []
                for t in (tile, tile + tiles // 2):
                    rate = rate_buf[int(heat), layer // shared, t, xi // 8]
                    c = f_buf[layer, t, 0, at, :]
                    h = f_buf[layer, t, 1, at, :]
                    if heat:
                        c2 = c * c
                        value = h + rate * c2 / (1.0 + c2)
                        if layer == 0:
                            value = value - sink_buf[t, xi // 16] * (h + 1.0)
                    else:
                        value = c + rate * jnp.tanh(h - c)
                    rhs.append(value)
                rows = pl.ds((layer * steps + xi) * SUB, SUB)
                cols = pl.ds(tile * LANES, LANES)
                sums[rows, cols] = rhs[0] + rhs[1]
                diffs[rows, cols] = rhs[0] - rhs[1]

    def forward_y(g, tables_y, sums, diffs, modes, outs):
        eh, el, oh, ol = tables_y
        for parity, (src, hi, lo) in enumerate(((sums, eh, el), (diffs, oh, ol))):
            both = dot3(src[...], hi[...], lo[...], ((1,), (0,)))
            for chunk in range(chunks // 2):
                part = both[:, chunk * lanes : (chunk + 1) * lanes]
                modes[parity * (chunks // 2) + chunk] = part.reshape(piece)
        for j in range(chunks):
            outs[j][...] = modes[(g // 2) ^ j]

    def first_kernel(rates_hbm, eig_hbm, f_hbm, id_hbm, mask_hbm, *rest):
        tables_hbm, outs = rest[:4], rest[4 : 4 + chunks]
        f_buf, rate_buf, sink_buf = rest[4 + chunks : 7 + chunks]
        tables_y = rest[7 + chunks : 11 + chunks]
        decay_ref, gain_ref, up_ref, down_ref, weight_ref = rest[11 + chunks : 16 + chunks]
        id_buf, mask_buf, sums, diffs, modes, rates, eig_ref = rest[16 + chunks : -4]
        f_sems, id_sems, mask_sems, table_sems = rest[-4:]
        g = lax.axis_index("gz")
        field = g % 2
        rate_copy = pltpu.make_async_copy(rates_hbm, rates, table_sems.at[4])
        id_copies = [
            [
                pltpu.make_async_copy(
                    id_hbm.at[group * shared, :, pl.ds(t * LANES, LANES)],
                    id_buf.at[group, t],
                    id_sems.at[group, t],
                )
                for group in range(depth // shared)
            ]
            for t in range(tiles)
        ]
        mask_copies = [
            pltpu.make_async_copy(
                mask_hbm.at[:, pl.ds(t * LANES, LANES)], mask_buf.at[t], mask_sems.at[t]
            )
            for t in range(tiles)
        ]
        field_copies = [
            [
                pltpu.make_async_copy(
                    f_hbm.at[:, layer, :, pl.ds(t * LANES, LANES)],
                    f_buf.at[layer, t],
                    f_sems.at[layer, t],
                )
                for layer in range(depth)
            ]
            for t in range(tiles)
        ]
        table_copies = [
            pltpu.make_async_copy(tables_hbm[i], tables_y[i], table_sems.at[i]) for i in range(4)
        ]
        eig_copy = pltpu.make_async_copy(eig_hbm, eig_ref, table_sems.at[5])
        eig_copy.start()
        rate_copy.start()
        for copies in id_copies:
            for copy in copies:
                copy.start()

        @pl.when(g == 0)
        def _():
            for copy in mask_copies:
                copy.start()

        for tile in range(tiles // 2):
            for t in (tile, tile + tiles // 2):
                for copy in field_copies[t]:
                    copy.start()
        for copy in table_copies:
            copy.start()
        eig_copy.wait()
        spread = jnp.where(g % 2 == 0, spread_solute, spread_heat).astype(f32)
        eig_one = eig_ref[pl.ds(g // 2, 1), :]
        eig_rows = jnp.broadcast_to(eig_one, (SUB, lanes))
        row = lax.broadcasted_iota(jnp.int32, (SUB, lanes), 0)
        for k in range(layers):
            decay, root = line_factors(eig_rows, spread, layer_eig[k])
            step_decay = power(decay, steps)
            decay_ref[k] = decay
            gain_ref[k] = ((1.0 if k == 0 else 2.0) / layers) / root
            up_ref[k] = sublane_powers(step_decay, row, False)
            down_ref[k] = sublane_powers(step_decay, row, True)
            block_decay = power(decay[:1], local_x)
            weight = jnp.ones_like(block_decay)
            for m in range(devices_x):
                weight_ref[m, pl.ds(k, 1), :] = weight
                weight = weight * block_decay
            for m in range(devices_x):
                weight_ref[m, pl.ds(k, 1), :] = weight_ref[m, pl.ds(k, 1), :] / (1.0 - weight)
        rate_copy.wait()
        for copies in id_copies:
            for copy in copies:
                copy.wait()
        for group in range(depth // shared):
            for t in range(tiles):
                for run in range(grain_runs):
                    ids = id_buf[group, t, pl.ds(run * 8, SUB, stride=steps), :]
                    found = [jnp.zeros(ids.shape, f32)] * 2
                    for grain in range(grain_count):
                        hit = ids == grain
                        found = [jnp.where(hit, rates[f, grain], found[f]) for f in range(2)]
                    for f in range(2):
                        rate_buf[f, group, t, run] = found[f]

        @pl.when(g == 0)
        def _():
            for copy in mask_copies:
                copy.wait()
            for t in range(tiles):
                for run in range(mask_runs):
                    mask = mask_buf[t, pl.ds(run * 16, SUB, stride=steps), :]
                    sink_buf[t, run] = mask.astype(f32) * heat_loss

        @pl.when(g != 0)
        def _():
            sink_buf[...] = jnp.zeros_like(sink_buf)

        for tile in range(tiles // 2):
            for t in (tile, tile + tiles // 2):
                for copy in field_copies[t]:
                    copy.wait()
            for heat in (False, True):
                pl.when(field == int(heat))(
                    functools.partial(fill, heat, tile, f_buf, rate_buf, sink_buf, sums, diffs)
                )
        for copy in table_copies:
            copy.wait()
        forward_y(g, tables_y, sums, diffs, modes, outs)

    def second_kernel(f_buf, rate_buf, sink_buf, *rest):
        tables_y, outs = rest[:4], rest[4 : 4 + chunks]
        sums, diffs, modes = rest[4 + chunks :]
        g = lax.axis_index("gz")
        for heat in (False, True):

            @pl.when(1 - g % 2 == int(heat))
            def _(heat=heat):
                for tile in range(tiles // 2):
                    fill(heat, tile, f_buf, rate_buf, sink_buf, sums, diffs)

        forward_y(g, tables_y, sums, diffs, modes, outs)

    piece_shapes = [jax.ShapeDtypeStruct(piece, f32)] * chunks
    work_scratch = [
        pltpu.VMEM((depth * local_x, half), f32),
        pltpu.VMEM((depth * local_x, half), f32),
        pltpu.VMEM((chunks,) + piece, f32),
    ]
    first_out = pl.pallas_call(
        first_kernel,
        in_specs=[hbm] * 9,
        out_specs=[vmem] * (chunks + len(ahead) + len(factor_shapes)),
        out_shape=piece_shapes + list(ahead) + factor_shapes,
        scratch_shapes=[
            pltpu.VMEM((depth // shared, tiles, local_x, LANES), jnp.int32),
            pltpu.VMEM((tiles, local_x, LANES), jnp.int32),
            *work_scratch,
            pltpu.SMEM((2, grain_count), f32),
            pltpu.VMEM((chunks, lanes), f32),
            pltpu.SemaphoreType.DMA((depth, tiles)),
            pltpu.SemaphoreType.DMA((depth // shared, tiles)),
            pltpu.SemaphoreType.DMA((tiles,)),
            pltpu.SemaphoreType.DMA((6,)),
        ],
        compiler_params=params,
        name="sources_own",
    )(
        *(
            pltpu.with_memory_space_constraint(a, pltpu.HBM)
            for a in (grain_rates.T, eig_table, fields, grain_ids, die_mask, *tables)
        )
    )
    own_pieces = first_out[:chunks]
    other_pieces = pl.pallas_call(
        second_kernel,
        in_specs=[vmem] * len(ahead),
        out_specs=[vmem] * chunks,
        out_shape=piece_shapes,
        scratch_shapes=work_scratch,
        compiler_params=params,
        cost_estimate=cover,
        name="sources_other",
    )(*first_out[chunks : chunks + len(ahead)])
    decays, gains, ups, downs, weights = first_out[chunks + len(ahead) :]
    pieces = [(own_pieces, other_pieces)[k % 2][k // 2] for k in range(devices_z)]

    def exchange(arrays, axis, order):
        count = lax.axis_size(axis)
        out = []
        for k in order:
            route = [(i, i ^ k) for i in range(count)]
            out.append(lax.ppermute(arrays[k], axis, route) if k else arrays[k])
        return out

    order_own = [0] + list(range(1, chunks))[::-1]
    order_other = list(range(chunks))[::-1]
    order_z = [2 * j for j in order_own] + [2 * j + 1 for j in order_other]
    order_x = list(range(devices_x))

    gathered = exchange(pieces, "gz", order_z)

    def gather_kernel(decay_ref, up_ref, down_ref, *rest):
        ins = rest[:devices_z]
        hat_ref, left_ref, right_ref, ends, field = rest[devices_z:]
        g = lax.axis_index("gz")
        for i, k in enumerate(order_z):
            field[pl.ds((g ^ k) * depth, depth)] = ins[i][...]

        def transform(xi, carry):
            hat = cosine_forward([field[z, xi] for z in range(layers)])
            for k in range(layers):
                hat_ref[k, xi] = hat[k]
            return carry

        lax.fori_loop(0, steps, transform, 0, unroll=4)
        for k in range(layers):
            decay = decay_ref[k]
            left = hat_ref[k, 0]
            right = hat_ref[k, steps - 1]
            for xi in range(1, steps):
                left = hat_ref[k, xi] + decay * left
                right = hat_ref[k, steps - 1 - xi] + decay * right
            ends[0, pl.ds(k, 1), :] = jnp.sum(left * down_ref[k], axis=0, keepdims=True)
            ends[1, pl.ds(k, 1), :] = jnp.sum(right * up_ref[k], axis=0, keepdims=True)
            left_ref[k] = left
            right_ref[k] = right

    hat, lefts, rights, ends = pl.pallas_call(
        gather_kernel,
        in_specs=[vmem] * (3 + devices_z),
        out_specs=[vmem] * 4,
        out_shape=[
            jax.ShapeDtypeStruct((layers, steps, SUB, lanes), f32),
            per_run,
            per_run,
            jax.ShapeDtypeStruct((2, layers, lanes), f32),
        ],
        scratch_shapes=[pltpu.VMEM((layers, steps, SUB, lanes), f32)],
        compiler_params=params,
        name="gather",
    )(decays, ups, downs, *gathered)

    def carry_kernel(decay_ref, left_ref, right_ref, from_left, from_right):
        row = lax.broadcasted_iota(jnp.int32, (SUB, lanes), 0)
        for k in range(layers):
            factor = power(decay_ref[k], steps)
            left = jnp.where(row >= 1, pltpu.roll(left_ref[k], 1, 0), 0.0)
            right = jnp.where(row < SUB - 1, pltpu.roll(right_ref[k], SUB - 1, 0), 0.0)
            for shift in (1, 2, 4):
                left = left + factor * jnp.where(row >= shift, pltpu.roll(left, shift, 0), 0.0)
                right = right + factor * jnp.where(
                    row < SUB - shift, pltpu.roll(right, SUB - shift, 0), 0.0
                )
                factor = factor * factor
            from_left[k] = left
            from_right[k] = right

    from_left, from_right = pl.pallas_call(
        carry_kernel,
        in_specs=[vmem] * 3,
        out_specs=[vmem] * 2,
        out_shape=[per_run] * 2,
        compiler_params=params,
        cost_estimate=cover,
        name="carry",
    )(decays, lefts, rights)

    all_ends = exchange([ends] * devices_x, "gx", order_x)

    def solve_kernel(decay_ref, gain_ref, up_ref, down_ref, weight_ref, hat_ref, left_ref, right_ref, *rest):
        end_refs = rest[:devices_x]
        outs = rest[devices_x : devices_x + devices_z]
        near, work, entry = rest[devices_x + devices_z :]
        g = lax.axis_index("gz")
        place = lax.axis_index("gx")
        for i, k in enumerate(order_x):
            near[place ^ k] = end_refs[i][...]
        for direction in range(2):
            total = None
            for m in range(1, devices_x + 1):
                shift = m if direction else devices_x - m
                value = weight_ref[m - 1] * near[(place + shift) % devices_x, direction]
                total = value if total is None else total + value
            entry[direction] = total
        for k in range(layers):
            decay, gain = decay_ref[k], gain_ref[k]
            left = left_ref[k] + up_ref[k] * entry[0, pl.ds(k, 1), :]
            right = right_ref[k] + down_ref[k] * entry[1, pl.ds(k, 1), :]
            for xi in range(steps):
                left = hat_ref[k, xi] + decay * left
                work[k, xi] = left
            for xi in reversed(range(steps)):
                carried = decay * right
                work[k, xi] = gain * (work[k, xi] + carried)
                right = hat_ref[k, xi] + carried

        def back(xi, carry):
            values = cosine_backward([work[k, xi] for k in range(layers)])
            for z in range(layers):
                work[z, xi] = values[z]
            return carry

        lax.fori_loop(0, steps, back, 0, unroll=4)
        for k in range(devices_z):
            outs[k][...] = work[pl.ds((g ^ k) * depth, depth)]

    solved = pl.pallas_call(
        solve_kernel,
        in_specs=[vmem] * (8 + devices_x),
        out_specs=[vmem] * devices_z,
        out_shape=[jax.ShapeDtypeStruct(piece, f32)] * devices_z,
        scratch_shapes=[
            pltpu.VMEM((devices_x, 2, layers, lanes), f32),
            pltpu.VMEM((layers, steps, SUB, lanes), f32),
            pltpu.VMEM((2, layers, lanes), f32),
        ],
        compiler_params=params,
        name="solve",
    )(decays, gains, ups, downs, weights, hat, from_left, from_right, *all_ends)

    returned = exchange(solved, "gz", order_z)

    def backward_y(tables_y, order, ins, modes, buf, done):
        eh, el, oh, ol = tables_y
        g = lax.axis_index("gz")
        for i, j in enumerate(order):
            modes[(g // 2) ^ j] = ins[i][...]
        dims = ((1,), (0,))
        for layer in range(depth):
            parts = [modes[chunk, layer].reshape(local_x, lanes) for chunk in range(chunks)]
            low = dot3(jnp.concatenate(parts[: chunks // 2], axis=1), eh[...], el[...], dims)
            high = dot3(jnp.concatenate(parts[chunks // 2 :], axis=1), oh[...], ol[...], dims)
            for side, value in enumerate((low + high, low - high)):
                for col in range(tiles // 2):
                    t = side * (tiles // 2) + col
                    for xi in range(steps):
                        at = xi * SUB
                        buf[layer, t, pl.ds(xi, SUB, stride=steps), :] = value[
                            at : at + SUB, col * LANES : (col + 1) * LANES
                        ]
                    done(layer, t)

    def own_kernel(*refs):
        buf, modes = refs[4 + chunks :]
        backward_y(refs[:4], order_own, refs[4 : 4 + chunks], modes, buf, lambda layer, t: None)

    def other_kernel(own_buf, *refs):
        out_ref, modes, buf, own_sems, sems = refs[4 + chunks :]
        mine = lax.axis_index("gz") % 2
        copies = []

        def send(source, field, layer, t, sem):
            copies.append(
                pltpu.make_async_copy(
                    source.at[layer, t], out_ref.at[field, layer, :, pl.ds(t * LANES, LANES)], sem
                )
            )
            copies[-1].start()

        for layer in range(depth):
            for t in range(tiles):
                send(own_buf, mine, layer, t, own_sems.at[layer, t])
        backward_y(
            refs[:4],
            order_other,
            refs[4 : 4 + chunks],
            modes,
            buf,
            lambda layer, t: send(buf, 1 - mine, layer, t, sems.at[layer, t]),
        )
        for copy in copies:
            copy.wait()

    by_source = dict(zip(order_z, returned))
    buffer = (depth, tiles, local_x, LANES)
    modes_scratch = pltpu.VMEM((chunks,) + piece, f32)
    own_buf = pl.pallas_call(
        own_kernel,
        in_specs=[vmem] * (4 + chunks),
        out_specs=vmem,
        out_shape=jax.ShapeDtypeStruct(buffer, f32),
        scratch_shapes=[modes_scratch],
        compiler_params=params,
        cost_estimate=cover,
        name="finish_own",
    )(*back_tables, *(by_source[2 * j] for j in order_own))
    tile_sems = pltpu.SemaphoreType.DMA((depth, tiles))
    return pl.pallas_call(
        other_kernel,
        in_specs=[vmem] * (5 + chunks),
        out_specs=hbm,
        out_shape=jax.ShapeDtypeStruct((2, depth, local_x, span_y), f32),
        scratch_shapes=[modes_scratch, pltpu.VMEM(buffer, f32), tile_sems, tile_sems],
        compiler_params=params,
        name="finish_other",
    )(own_buf, *back_tables, *(by_source[2 * j + 1] for j in order_other))


def solution(mesh):
    placed = (P(None, "gz", "gx", None), P("gz", "gx", None), P(), P("gx", None))
    return jax.shard_map(
        on_device_fn, mesh=mesh, in_specs=placed, out_specs=P(None, "gz", "gx", None), check_vma=False
    )
```

```python
import functools
import math

import numpy as np
import jax
import jax.numpy as jnp
from jax import lax
from jax.experimental import pallas as pl
from jax.experimental.pallas import tpu as pltpu
from jax.sharding import PartitionSpec as P

heat_loss = 4.0
spread_solute = 2.0
spread_heat = 100.0
SUB = 8
LANES = 128
VMEM_LIMIT = 48 * 1024 * 1024


def split_tables(n):
    half = n // 2
    y = np.arange(half)
    cols, freq = [], []
    for j in range(half // 2 + 1):
        k = 2 * j
        scale = math.sqrt((1.0 if k in (0, half) else 2.0) / n)
        cols.append(scale * np.cos(2 * np.pi * k * y / n))
        freq.append(k)
        if 0 < j < half // 2:
            cols.append(scale * np.sin(2 * np.pi * k * y / n))
            freq.append(k)
    even = np.stack(cols, 1)
    cols, odd_freq = [], []
    for j in range(half // 2):
        k = 2 * j + 1
        scale = math.sqrt(2.0 / n)
        cols.append(scale * np.cos(2 * np.pi * k * y / n))
        cols.append(scale * np.sin(2 * np.pi * k * y / n))
        odd_freq += [k, k]
    odd = np.stack(cols, 1)
    eig = 4.0 * np.sin(np.pi * np.array(freq + odd_freq) / n) ** 2
    return even, odd, eig.astype(np.float32)


def hi_lo(a):
    hi = jnp.asarray(a, jnp.float32).astype(jnp.bfloat16)
    lo = (jnp.asarray(a, jnp.float32) - hi.astype(jnp.float32)).astype(jnp.bfloat16)
    return hi, lo


def table_pair(a):
    bf16 = jnp.bfloat16
    hi = a.astype(np.float32).astype(bf16)
    lo = (a - hi.astype(np.float64)).astype(np.float32).astype(bf16)
    return hi, lo


def dot3(x, q_hi, q_lo, dims):
    hi, lo = hi_lo(x)
    dn = (dims, ((), ()))
    f32 = jnp.float32
    return (
        lax.dot_general(hi, q_hi, dn, preferred_element_type=f32)
        + lax.dot_general(hi, q_lo, dn, preferred_element_type=f32)
        + lax.dot_general(lo, q_hi, dn, preferred_element_type=f32)
    )


def cosine_forward(v):
    n = len(v)
    if n == 1:
        return [v[0]]
    h = n // 2
    sums = [v[z] + v[n - 1 - z] for z in range(h)]
    diffs = [v[z] - v[n - 1 - z] for z in range(h)]
    even = cosine_forward(sums)
    out = [None] * n
    for j in range(h):
        out[2 * j] = even[j]
        k = 2 * j + 1
        acc = None
        for z in range(h):
            term = diffs[z] * float(math.cos(math.pi * k * (z + 0.5) / n))
            acc = term if acc is None else acc + term
        out[k] = acc
    return out


def cosine_backward(c):
    n = len(c)
    if n == 1:
        return [c[0]]
    h = n // 2
    even = cosine_backward([c[2 * j] for j in range(h)])
    out = [None] * n
    for z in range(h):
        acc = None
        for j in range(h):
            k = 2 * j + 1
            term = c[k] * float(math.cos(math.pi * k * (z + 0.5) / n))
            acc = term if acc is None else acc + term
        out[z] = even[z] + acc
        out[n - 1 - z] = even[z] - acc
    return out


def line_factors(eig_rows, spread, layer_eig):
    rest = 1.0 + spread * (eig_rows + layer_eig)
    root = jnp.sqrt(rest * (rest + 4.0 * spread))
    decay = 2.0 * spread / (rest + 2.0 * spread + root)
    return decay, root


def power(base, exponent):
    out = None
    square = base
    while exponent:
        if exponent & 1:
            out = square if out is None else out * square
        exponent >>= 1
        if exponent:
            square = square * square
    return out


def sublane_powers(step_decay, row, reverse):
    out = jnp.ones_like(step_decay)
    factor = step_decay
    place = (SUB - 1 - row) if reverse else row
    for bit in range(3):
        out = jnp.where((place >> bit) & 1 == 1, out * factor, out)
        factor = factor * factor
    return out


def on_device_fn(fields, grain_ids, grain_rates, die_mask):
    depth = fields.shape[1]
    local_x = fields.shape[2]
    span_y = fields.shape[3]
    half = span_y // 2
    devices_x = lax.axis_size("gx")
    devices_z = lax.axis_size("gz")
    layers = depth * devices_z
    chunks = devices_z // 2
    lanes = span_y // chunks
    steps = local_x // SUB
    tiles = span_y // LANES
    grain_count = grain_rates.shape[0]
    even, odd, eig = split_tables(span_y)
    even_hi, even_lo = table_pair(even)
    odd_hi, odd_lo = table_pair(odd)
    tables = [jnp.asarray(t) for t in (even_hi, even_lo, odd_hi, odd_lo)]
    back_tables = [jnp.asarray(np.ascontiguousarray(t.T)) for t in (even_hi, even_lo, odd_hi, odd_lo)]
    eig_table = jnp.asarray(eig.reshape(chunks, lanes))
    f32 = jnp.float32
    cover = pl.CostEstimate(flops=8 * 10**9, transcendentals=0, bytes_accessed=24 * 10**6)
    params = pltpu.CompilerParams(vmem_limit_bytes=VMEM_LIMIT)
    piece = (depth, steps, SUB, lanes)
    grain_run = min(steps, 8)
    mask_run = min(steps, 16)

    vmem = pl.BlockSpec(memory_space=pltpu.VMEM)
    hbm = pl.BlockSpec(memory_space=pltpu.HBM)
    shared = 2 if depth % 2 == 0 else 1

    grain_runs = max(steps // 8, 1)
    mask_runs = max(steps // 16, 1)
    ahead = (
        jax.ShapeDtypeStruct((depth, tiles, 2, local_x, LANES), f32),
        jax.ShapeDtypeStruct((2, depth // shared, tiles, grain_runs, SUB, LANES), f32),
        jax.ShapeDtypeStruct((tiles, mask_runs, SUB, LANES), f32),
    ) + tuple(jax.ShapeDtypeStruct((half, half), jnp.bfloat16) for _ in range(4))

    layer_eig = [4.0 * math.sin(math.pi * k / (2 * layers)) ** 2 for k in range(layers)]
    per_run = jax.ShapeDtypeStruct((layers, SUB, lanes), f32)
    factor_shapes = [per_run] * 4 + [jax.ShapeDtypeStruct((devices_x, layers, lanes), f32)]

    def fill(heat, tile, f_buf, rate_buf, sink_buf, sums, diffs):
        for xi in range(steps):
            at = pl.ds(xi, SUB, stride=steps)
            for layer in range(depth):
                rhs = []
                for t in (tile, tile + tiles // 2):
                    rate = rate_buf[int(heat), layer // shared, t, xi // 8]
                    c = f_buf[layer, t, 0, at, :]
                    h = f_buf[layer, t, 1, at, :]
                    if heat:
                        c2 = c * c
                        value = h + rate * c2 / (1.0 + c2)
                        if layer == 0:
                            value = value - sink_buf[t, xi // 16] * (h + 1.0)
                    else:
                        value = c + rate * jnp.tanh(h - c)
                    rhs.append(value)
                rows = pl.ds((layer * steps + xi) * SUB, SUB)
                cols = pl.ds(tile * LANES, LANES)
                sums[rows, cols] = rhs[0] + rhs[1]
                diffs[rows, cols] = rhs[0] - rhs[1]

    def forward_y(g, tables_y, sums, diffs, modes, outs):
        eh, el, oh, ol = tables_y
        for parity, (src, hi, lo) in enumerate(((sums, eh, el), (diffs, oh, ol))):
            both = dot3(src[...], hi[...], lo[...], ((1,), (0,)))
            for chunk in range(chunks // 2):
                part = both[:, chunk * lanes : (chunk + 1) * lanes]
                modes[parity * (chunks // 2) + chunk] = part.reshape(piece)
        for j in range(chunks):
            outs[j][...] = modes[(g // 2) ^ j]

    def first_kernel(rates_hbm, eig_hbm, f_hbm, id_hbm, mask_hbm, *rest):
        tables_hbm, outs = rest[:4], rest[4 : 4 + chunks]
        f_buf, rate_buf, sink_buf = rest[4 + chunks : 7 + chunks]
        tables_y = rest[7 + chunks : 11 + chunks]
        decay_ref, gain_ref, up_ref, down_ref, weight_ref = rest[11 + chunks : 16 + chunks]
        id_buf, mask_buf, sums, diffs, modes, rates, eig_ref = rest[16 + chunks : -4]
        f_sems, id_sems, mask_sems, table_sems = rest[-4:]
        g = lax.axis_index("gz")
        field = g % 2
        rate_copy = pltpu.make_async_copy(rates_hbm, rates, table_sems.at[4])
        id_copies = [
            [
                pltpu.make_async_copy(
                    id_hbm.at[group * shared, :, pl.ds(t * LANES, LANES)],
                    id_buf.at[group, t],
                    id_sems.at[group, t],
                )
                for group in range(depth // shared)
            ]
            for t in range(tiles)
        ]
        mask_copies = [
            pltpu.make_async_copy(
                mask_hbm.at[:, pl.ds(t * LANES, LANES)], mask_buf.at[t], mask_sems.at[t]
            )
            for t in range(tiles)
        ]
        field_copies = [
            [
                pltpu.make_async_copy(
                    f_hbm.at[:, layer, :, pl.ds(t * LANES, LANES)],
                    f_buf.at[layer, t],
                    f_sems.at[layer, t],
                )
                for layer in range(depth)
            ]
            for t in range(tiles)
        ]
        table_copies = [
            pltpu.make_async_copy(tables_hbm[i], tables_y[i], table_sems.at[i]) for i in range(4)
        ]
        eig_copy = pltpu.make_async_copy(eig_hbm, eig_ref, table_sems.at[5])
        eig_copy.start()
        rate_copy.start()
        for copies in id_copies:
            for copy in copies:
                copy.start()

        @pl.when(g == 0)
        def _():
            for copy in mask_copies:
                copy.start()

        for tile in range(tiles // 2):
            for t in (tile, tile + tiles // 2):
                for copy in field_copies[t]:
                    copy.start()
        for copy in table_copies:
            copy.start()
        eig_copy.wait()
        spread = jnp.where(g % 2 == 0, spread_solute, spread_heat).astype(f32)
        eig_one = eig_ref[pl.ds(g // 2, 1), :]
        eig_rows = jnp.broadcast_to(eig_one, (SUB, lanes))
        row = lax.broadcasted_iota(jnp.int32, (SUB, lanes), 0)
        for k in range(layers):
            decay, root = line_factors(eig_rows, spread, layer_eig[k])
            step_decay = power(decay, steps)
            decay_ref[k] = decay
            gain_ref[k] = ((1.0 if k == 0 else 2.0) / layers) / root
            up_ref[k] = sublane_powers(step_decay, row, False)
            down_ref[k] = sublane_powers(step_decay, row, True)
            block_decay = power(decay[:1], local_x)
            weight = jnp.ones_like(block_decay)
            for m in range(devices_x):
                weight_ref[m, pl.ds(k, 1), :] = weight
                weight = weight * block_decay
            for m in range(devices_x):
                weight_ref[m, pl.ds(k, 1), :] = weight_ref[m, pl.ds(k, 1), :] / (1.0 - weight)
        rate_copy.wait()
        for copies in id_copies:
            for copy in copies:
                copy.wait()
        for group in range(depth // shared):
            for t in range(tiles):
                for run in range(grain_runs):
                    ids = id_buf[group, t, pl.ds(run * 8, SUB, stride=steps), :]
                    found = [jnp.zeros(ids.shape, f32)] * 2
                    for grain in range(grain_count):
                        hit = ids == grain
                        found = [jnp.where(hit, rates[f, grain], found[f]) for f in range(2)]
                    for f in range(2):
                        rate_buf[f, group, t, run] = found[f]

        @pl.when(g == 0)
        def _():
            for copy in mask_copies:
                copy.wait()
            for t in range(tiles):
                for run in range(mask_runs):
                    mask = mask_buf[t, pl.ds(run * 16, SUB, stride=steps), :]
                    sink_buf[t, run] = mask.astype(f32) * heat_loss

        @pl.when(g != 0)
        def _():
            sink_buf[...] = jnp.zeros_like(sink_buf)

        for tile in range(tiles // 2):
            for t in (tile, tile + tiles // 2):
                for copy in field_copies[t]:
                    copy.wait()
            for heat in (False, True):
                pl.when(field == int(heat))(
                    functools.partial(fill, heat, tile, f_buf, rate_buf, sink_buf, sums, diffs)
                )
        for copy in table_copies:
            copy.wait()
        forward_y(g, tables_y, sums, diffs, modes, outs)

    def second_kernel(f_buf, rate_buf, sink_buf, *rest):
        tables_y, outs = rest[:4], rest[4 : 4 + chunks]
        sums, diffs, modes = rest[4 + chunks :]
        g = lax.axis_index("gz")
        for heat in (False, True):

            @pl.when(1 - g % 2 == int(heat))
            def _(heat=heat):
                for tile in range(tiles // 2):
                    fill(heat, tile, f_buf, rate_buf, sink_buf, sums, diffs)

        forward_y(g, tables_y, sums, diffs, modes, outs)

    piece_shapes = [jax.ShapeDtypeStruct(piece, f32)] * chunks
    work_scratch = [
        pltpu.VMEM((depth * local_x, half), f32),
        pltpu.VMEM((depth * local_x, half), f32),
        pltpu.VMEM((chunks,) + piece, f32),
    ]
    first_out = pl.pallas_call(
        first_kernel,
        in_specs=[hbm] * 9,
        out_specs=[vmem] * (chunks + len(ahead) + len(factor_shapes)),
        out_shape=piece_shapes + list(ahead) + factor_shapes,
        scratch_shapes=[
            pltpu.VMEM((depth // shared, tiles, local_x, LANES), jnp.int32),
            pltpu.VMEM((tiles, local_x, LANES), jnp.int32),
            *work_scratch,
            pltpu.SMEM((2, grain_count), f32),
            pltpu.VMEM((chunks, lanes), f32),
            pltpu.SemaphoreType.DMA((depth, tiles)),
            pltpu.SemaphoreType.DMA((depth // shared, tiles)),
            pltpu.SemaphoreType.DMA((tiles,)),
            pltpu.SemaphoreType.DMA((6,)),
        ],
        compiler_params=params,
        name="sources_own",
    )(
        *(
            pltpu.with_memory_space_constraint(a, pltpu.HBM)
            for a in (grain_rates.T, eig_table, fields, grain_ids, die_mask, *tables)
        )
    )
    own_pieces = first_out[:chunks]
    other_pieces = pl.pallas_call(
        second_kernel,
        in_specs=[vmem] * len(ahead),
        out_specs=[vmem] * chunks,
        out_shape=piece_shapes,
        scratch_shapes=work_scratch,
        compiler_params=params,
        cost_estimate=cover,
        name="sources_other",
    )(*first_out[chunks : chunks + len(ahead)])
    decays, gains, ups, downs, weights = first_out[chunks + len(ahead) :]
    pieces = [(own_pieces, other_pieces)[k % 2][k // 2] for k in range(devices_z)]

    def exchange(arrays, axis, order):
        count = lax.axis_size(axis)
        out = []
        for k in order:
            route = [(i, i ^ k) for i in range(count)]
            out.append(lax.ppermute(arrays[k], axis, route) if k else arrays[k])
        return out

    order_own = [0, chunks - 1] + list(range(1, chunks - 1))
    order_other = list(range(chunks))[::-1]
    order_z = [2 * j for j in order_own] + [2 * j + 1 for j in order_other]
    order_x = list(range(devices_x))

    gathered = exchange(pieces, "gz", order_z)

    def gather_kernel(decay_ref, up_ref, down_ref, *rest):
        ins = rest[:devices_z]
        hat_ref, left_ref, right_ref, ends, field = rest[devices_z:]
        g = lax.axis_index("gz")
        for i, k in enumerate(order_z):
            field[pl.ds((g ^ k) * depth, depth)] = ins[i][...]

        def transform(xi, carry):
            hat = cosine_forward([field[z, xi] for z in range(layers)])
            for k in range(layers):
                hat_ref[k, xi] = hat[k]
            return carry

        lax.fori_loop(0, steps, transform, 0, unroll=4)
        for k in range(layers):
            decay = decay_ref[k]
            left = hat_ref[k, 0]
            right = hat_ref[k, steps - 1]
            for xi in range(1, steps):
                left = hat_ref[k, xi] + decay * left
                right = hat_ref[k, steps - 1 - xi] + decay * right
            ends[0, pl.ds(k, 1), :] = jnp.sum(left * down_ref[k], axis=0, keepdims=True)
            ends[1, pl.ds(k, 1), :] = jnp.sum(right * up_ref[k], axis=0, keepdims=True)
            left_ref[k] = left
            right_ref[k] = right

    hat, lefts, rights, ends = pl.pallas_call(
        gather_kernel,
        in_specs=[vmem] * (3 + devices_z),
        out_specs=[vmem] * 4,
        out_shape=[
            jax.ShapeDtypeStruct((layers, steps, SUB, lanes), f32),
            per_run,
            per_run,
            jax.ShapeDtypeStruct((2, layers, lanes), f32),
        ],
        scratch_shapes=[pltpu.VMEM((layers, steps, SUB, lanes), f32)],
        compiler_params=params,
        name="gather",
    )(decays, ups, downs, *gathered)

    def carry_kernel(decay_ref, left_ref, right_ref, from_left, from_right):
        row = lax.broadcasted_iota(jnp.int32, (SUB, lanes), 0)
        for k in range(layers):
            factor = power(decay_ref[k], steps)
            left = jnp.where(row >= 1, pltpu.roll(left_ref[k], 1, 0), 0.0)
            right = jnp.where(row < SUB - 1, pltpu.roll(right_ref[k], SUB - 1, 0), 0.0)
            for shift in (1, 2, 4):
                left = left + factor * jnp.where(row >= shift, pltpu.roll(left, shift, 0), 0.0)
                right = right + factor * jnp.where(
                    row < SUB - shift, pltpu.roll(right, SUB - shift, 0), 0.0
                )
                factor = factor * factor
            from_left[k] = left
            from_right[k] = right

    from_left, from_right = pl.pallas_call(
        carry_kernel,
        in_specs=[vmem] * 3,
        out_specs=[vmem] * 2,
        out_shape=[per_run] * 2,
        compiler_params=params,
        cost_estimate=cover,
        name="carry",
    )(decays, lefts, rights)

    all_ends = exchange([ends] * devices_x, "gx", order_x)

    def solve_kernel(decay_ref, gain_ref, up_ref, down_ref, weight_ref, hat_ref, left_ref, right_ref, *rest):
        end_refs = rest[:devices_x]
        outs = rest[devices_x : devices_x + devices_z]
        near, work, entry = rest[devices_x + devices_z :]
        g = lax.axis_index("gz")
        place = lax.axis_index("gx")
        for i, k in enumerate(order_x):
            near[place ^ k] = end_refs[i][...]
        for direction in range(2):
            total = None
            for m in range(1, devices_x + 1):
                shift = m if direction else devices_x - m
                value = weight_ref[m - 1] * near[(place + shift) % devices_x, direction]
                total = value if total is None else total + value
            entry[direction] = total
        for k in range(layers):
            decay, gain = decay_ref[k], gain_ref[k]
            left = left_ref[k] + up_ref[k] * entry[0, pl.ds(k, 1), :]
            right = right_ref[k] + down_ref[k] * entry[1, pl.ds(k, 1), :]
            for xi in range(steps):
                left = hat_ref[k, xi] + decay * left
                work[k, xi] = left
            for xi in reversed(range(steps)):
                carried = decay * right
                work[k, xi] = gain * (work[k, xi] + carried)
                right = hat_ref[k, xi] + carried

        def back(xi, carry):
            values = cosine_backward([work[k, xi] for k in range(layers)])
            for z in range(layers):
                work[z, xi] = values[z]
            return carry

        lax.fori_loop(0, steps, back, 0, unroll=4)
        for k in range(devices_z):
            outs[k][...] = work[pl.ds((g ^ k) * depth, depth)]

    solved = pl.pallas_call(
        solve_kernel,
        in_specs=[vmem] * (8 + devices_x),
        out_specs=[vmem] * devices_z,
        out_shape=[jax.ShapeDtypeStruct(piece, f32)] * devices_z,
        scratch_shapes=[
            pltpu.VMEM((devices_x, 2, layers, lanes), f32),
            pltpu.VMEM((layers, steps, SUB, lanes), f32),
            pltpu.VMEM((2, layers, lanes), f32),
        ],
        compiler_params=params,
        name="solve",
    )(decays, gains, ups, downs, weights, hat, from_left, from_right, *all_ends)

    returned = exchange(solved, "gz", order_z)

    def backward_y(tables_y, order, ins, modes, buf, done):
        eh, el, oh, ol = tables_y
        g = lax.axis_index("gz")
        for i, j in enumerate(order):
            modes[(g // 2) ^ j] = ins[i][...]
        dims = ((1,), (0,))
        parts = [modes[chunk].reshape(depth * local_x, lanes) for chunk in range(chunks)]
        low = dot3(jnp.concatenate(parts[: chunks // 2], axis=1), eh[...], el[...], dims)
        high = dot3(jnp.concatenate(parts[chunks // 2 :], axis=1), oh[...], ol[...], dims)
        for side, value in enumerate((low + high, low - high)):
            for layer in range(depth):
                for col in range(tiles // 2):
                    t = side * (tiles // 2) + col
                    for xi in range(steps):
                        at = (layer * steps + xi) * SUB
                        buf[layer, t, pl.ds(xi, SUB, stride=steps), :] = value[
                            at : at + SUB, col * LANES : (col + 1) * LANES
                        ]
                    done(layer, t)

    def own_kernel(*refs):
        buf, modes = refs[4 + chunks :]
        backward_y(refs[:4], order_own, refs[4 : 4 + chunks], modes, buf, lambda layer, t: None)

    def other_kernel(own_buf, *refs):
        out_ref, modes, buf, own_sems, sems = refs[4 + chunks :]
        mine = lax.axis_index("gz") % 2
        copies = []

        def send(source, field, layer, t, sem):
            copies.append(
                pltpu.make_async_copy(
                    source.at[layer, t], out_ref.at[field, layer, :, pl.ds(t * LANES, LANES)], sem
                )
            )
            copies[-1].start()

        for layer in range(depth):
            for t in range(tiles):
                send(own_buf, mine, layer, t, own_sems.at[layer, t])
        backward_y(
            refs[:4],
            order_other,
            refs[4 : 4 + chunks],
            modes,
            buf,
            lambda layer, t: send(buf, 1 - mine, layer, t, sems.at[layer, t]),
        )
        for copy in copies:
            copy.wait()

    by_source = dict(zip(order_z, returned))
    buffer = (depth, tiles, local_x, LANES)
    modes_scratch = pltpu.VMEM((chunks,) + piece, f32)
    own_buf = pl.pallas_call(
        own_kernel,
        in_specs=[vmem] * (4 + chunks),
        out_specs=vmem,
        out_shape=jax.ShapeDtypeStruct(buffer, f32),
        scratch_shapes=[modes_scratch],
        compiler_params=params,
        cost_estimate=cover,
        name="finish_own",
    )(*back_tables, *(by_source[2 * j] for j in order_own))
    tile_sems = pltpu.SemaphoreType.DMA((depth, tiles))
    return pl.pallas_call(
        other_kernel,
        in_specs=[vmem] * (5 + chunks),
        out_specs=hbm,
        out_shape=jax.ShapeDtypeStruct((2, depth, local_x, span_y), f32),
        scratch_shapes=[modes_scratch, pltpu.VMEM(buffer, f32), tile_sems, tile_sems],
        compiler_params=params,
        name="finish_other",
    )(own_buf, *back_tables, *(by_source[2 * j + 1] for j in order_other))


def solution(mesh):
    placed = (P(None, "gz", "gx", None), P("gz", "gx", None), P(), P("gx", None))
    return jax.shard_map(
        on_device_fn, mesh=mesh, in_specs=placed, out_specs=P(None, "gz", "gx", None), check_vma=False
    )
```
